32 devices in a mesh: run: 8 (over y, x, core), seg: 4 (over z).
Axes of the slice: x: 2, y: 2, z: 4, core: 2. Of those that a mesh axis runs over, the one named last changes fastest.
Arguments:
- diag_blocks: float32 [4, 16, 256, 256], P('seg', 'run'), as said below
- coupling: float32 [4, 16, 256, 256], P('seg', 'run')
- rhs: float32 [4, 16, 256, 128], P('seg', 'run'), may hold values from -0.65 to 0.65
Outputs:
- solution: float32 [4, 16, 256, 128], P('seg', 'run')
The draws below stay inside these ranges and needn't reach their ends.
Inputs may be any that keep to these rules, and one draw needn't show every extreme that they name: Together with coupling, diag_blocks makes A symmetric positive definite.
All inputs are finite; a program needn't handle non-finite values.
Results may differ from the reference program's by a relative error of at most 0.0003.
Values sent between devices are 32-bit elements; how exact they have to be, the bound alone decides.
A program may use at most 128 MiB of HBM per device.

```python
import math
import jax
import jax.numpy as jnp
from jax import lax

B = 256
R = 128
SEGMENTS = 4
SEG_SLABS = 16


def conductances(key):
    slab_total = SEGMENTS * SEG_SLABS
    noise_key = jax.random.fold_in(key, 7)
    noise_raw = jax.random.normal(noise_key, (slab_total, B, B), jnp.float32)
    gram_part = jnp.einsum('sij,skj->sik', noise_raw, noise_raw) / B
    return 0.5 * jnp.eye(B, dtype=jnp.float32) + 0.5 * gram_part


def draw_diag_blocks(key, part):
    slab_total = SEGMENTS * SEG_SLABS
    conduct = conductances(key)
    rolled = jnp.roll(conduct, -1, axis=0)
    log_low = math.log(0.001)
    log_high = math.log(0.01)
    masses = jnp.exp(jax.random.uniform(jax.random.fold_in(key, 9), (slab_total, B), jnp.float32, log_low, log_high))
    blocks = conduct + rolled + masses[:, :, None] * jnp.eye(B, dtype=jnp.float32)
    return blocks.reshape(SEGMENTS, SEG_SLABS, B, B)


def draw_coupling(key, part):
    return (-conductances(key)).reshape(SEGMENTS, SEG_SLABS, B, B)


def draw_rhs(key, part):
    slab_total = SEGMENTS * SEG_SLABS
    rough_key = jax.random.fold_in(key, 21)
    rough = jnp.clip(0.1 * jax.random.normal(rough_key, (slab_total, B, R), jnp.float32), -0.6, 0.6)
    amplitude = 0.003
    phase = jax.random.uniform(jax.random.fold_in(key, 22), (), jnp.float32, 0.0, 2.0 * math.pi)
    position = jnp.arange(slab_total, dtype=jnp.float32) / slab_total
    profile = 1.0 + 0.6 * jnp.cos(3.0 * math.pi * position + phase)
    weights = jax.random.uniform(jax.random.fold_in(key, 23), (1, B, R), jnp.float32, 0.5, 1.5)
    values = rough + amplitude * profile[:, None, None] * weights
    return values.reshape(SEGMENTS, SEG_SLABS, B, R)


def setup_inputs(seed: int = 0) -> dict:
    seeds = jax.random.split(jax.random.key(seed), 4)
    diag_blocks = draw_diag_blocks(jax.random.fold_in(seeds[3], 71), 0)
    coupling = draw_coupling(jax.random.fold_in(seeds[3], 71), 0)
    rhs = draw_rhs(jax.random.fold_in(seeds[3], 71), 0)
    return {"diag_blocks": diag_blocks, "coupling": coupling, "rhs": rhs}


HIGH = lax.Precision.HIGHEST

def product(operand, second):
    return jnp.dot(operand, second, precision=HIGH, preferred_element_type=operand.dtype)

def apply_inverse(factor, columns):
    return jax.scipy.linalg.cho_solve((factor, True), columns)

def reference(diag_blocks, coupling, rhs):
    order_b = diag_blocks.shape[-1]
    slab_total = diag_blocks.shape[0] * diag_blocks.shape[1]
    diagonal = diag_blocks.reshape(slab_total, order_b, order_b)
    couples = coupling.reshape(slab_total, order_b, order_b)
    couples = couples.at[0].set(jnp.zeros_like(couples[0]))
    sources = rhs.reshape(slab_total, order_b, rhs.shape[-1])
    couples_after = jnp.concatenate([couples[1:], jnp.zeros_like(couples[:1])], axis=0)

    def forward(state_now, slab_item):
        solved_link, solved_prev = state_now
        diag_here, coup_here, coup_next, source_here = slab_item
        factor = jnp.linalg.cholesky(diag_here - product(coup_here, solved_link))
        link_here = apply_inverse(factor, coup_next.T)
        value_here = apply_inverse(factor, source_here - product(coup_here, solved_prev))
        return ((link_here, value_here), (link_here, value_here))
    initial = (jnp.zeros_like(diagonal[0]), jnp.zeros_like(sources[0]))
    _, (links, partials) = lax.scan(forward, initial, (diagonal, couples, couples_after, sources))

    def backward(later, slab_item):
        link_here, partial_value = slab_item
        result = partial_value - product(link_here, later)
        return (result, result)
    _, values = lax.scan(backward, jnp.zeros_like(sources[0]), (links, partials), reverse=True)
    return values.reshape(rhs.shape)
```

```python
import functools

import jax
import jax.numpy as jnp
from jax import lax
from jax.experimental import pallas as pl
from jax.experimental.pallas import tpu as pltpu
from jax.sharding import PartitionSpec as P

MESH = pl.DeviceIdType.MESH
HIGH = lax.Precision.HIGHEST
ROWS = 8
GROUPS = 2
LANES = 128


def dot(a, b):
    return jnp.dot(a, b, precision=HIGH, preferred_element_type=jnp.float32)


def dot_nt(a, b):
    return lax.dot_general(
        a, b, (((1,), (1,)), ((), ())), precision=HIGH, preferred_element_type=jnp.float32
    )


def spread(x, shape):
    return jnp.broadcast_to(x, shape)


def total_of(terms):
    while len(terms) > 1:
        pairs = [terms[t] + terms[t + 1] for t in range(0, len(terms) - 1, 2)]
        terms = pairs + terms[len(pairs) * 2 :]
    return terms[0]


def three_parts(x):
    high = x.astype(jnp.bfloat16)
    rest = x - high.astype(jnp.float32)
    mid = rest.astype(jnp.bfloat16)
    low = (rest - mid.astype(jnp.float32)).astype(jnp.bfloat16)
    return [part.astype(jnp.float32) for part in (high, mid, low)]


def outer_product(left, right):
    lefts = list(zip(*[three_parts(x) for x in left]))
    rights = list(zip(*[three_parts(x) for x in right]))
    order = ((0, 0), (0, 1), (1, 0), (1, 1), (0, 2), (2, 0))
    stack = lambda parts, side: jnp.concatenate(
        [x for pair in order for x in parts[pair[side]]], axis=0
    ).astype(jnp.bfloat16)
    return lax.dot_general(
        stack(lefts, 0),
        stack(rights, 1),
        (((0,), (0,)), ((), ())),
        preferred_element_type=jnp.float32,
    )


def eliminate_panel(panel, first, sub, lane):
    shape = panel[0].shape
    groups = len(panel)
    width = groups * ROWS
    cols = [
        [jnp.where(lane >= 0, spread(p[:, first + j : first + j + 1], shape), 0.0) for p in panel]
        for j in range(width)
    ]
    for j in range(width):
        own, row = divmod(j, ROWS)
        here = sub == row
        inverse = 1.0 / spread(cols[j][own][row : row + 1, :], shape)
        factor = [jnp.where(here, -1.0, c) if i == own else c for i, c in enumerate(cols[j])]
        scaled = [f * inverse for f in factor]
        clear = lambda x, i: jnp.where(here, 0.0, x) if i == own else x
        for m in range(j + 1, width):
            line = spread(cols[m][own][row : row + 1, :], shape)
            if m == j + 1:
                steps = [(f * line) * inverse for f in factor]
            else:
                steps = [s * line for s in scaled]
            cols[m] = [clear(c, i) - steps[i] for i, c in enumerate(cols[m])]
        at = lane == first + j
        line = jnp.where(at, 1.0, spread(panel[own][row : row + 1, :], shape))
        panel = [
            clear(jnp.where(at, 0.0, p), i) - scaled[i] * line for i, p in enumerate(panel)
        ]
    return panel


def spd_inverse_tile(rows):
    shape = rows[0].shape
    sub = lax.broadcasted_iota(jnp.int32, shape, 0)
    lane = lax.broadcasted_iota(jnp.int32, shape, 1)
    rows = list(rows)
    width = GROUPS * ROWS
    for k in range(0, len(rows), GROUPS):
        first = k * ROWS
        inside = jnp.logical_and(lane >= first, lane < first + width)
        panel = rows[k : k + GROUPS]
        columns = [
            jnp.where(lane < first, -p, jnp.where(inside, 0.0, p)) for p in panel
        ]
        panel = eliminate_panel(panel, first, sub, lane)
        near = range(k + GROUPS, min(k + 2 * GROUPS, len(rows)))
        for i in near:
            terms = [
                spread(rows[i][:, first + j : first + j + 1], shape)
                * spread(panel[j // ROWS][j % ROWS : j % ROWS + 1, :], shape)
                for j in range(width)
            ]
            rows[i] = jnp.where(inside, 0.0, rows[i]) - total_of(terms)
        update = outer_product(columns, panel)
        for i in range(len(rows)):
            if i < k or i >= k + 2 * GROUPS:
                rows[i] = jnp.where(inside, 0.0, rows[i]) - update[i * ROWS : (i + 1) * ROWS, :]
        rows[k : k + GROUPS] = panel
    return rows


def invert(node, x, tile, work, late):
    half = tile.shape[0]
    top, low = slice(0, half), slice(half, 2 * half)
    tile[...] = node[0]

    @pl.loop(0, 2)
    def _(step):
        rows = spd_inverse_tile([tile[i : i + ROWS, :] for i in range(0, half, ROWS)])
        for i, row in enumerate(rows):
            tile[i * ROWS : (i + 1) * ROWS, :] = row

        @pl.when(step == 0)
        def _():
            late()
            x[top, top] = tile[...]
            work[0] = dot(tile[...], node[1])
            work[1] = work[0].T
            tile[...] = node[2] - dot(work[1], node[1])

        @pl.when(step == 1)
        def _():
            corner = -dot(tile[...], work[1])
            x[low, low] = tile[...]
            x[low, top] = corner
            x[top, low] = -dot(work[0], tile[...])
            x[top, top] = x[top, top] - dot(work[0], corner)


def kernel(
    runs,
    total,
    diag,
    coup,
    rhs,
    out,
    x,
    tile,
    work,
    node,
    source,
    e_turned,
    w_p,
    w_q,
    keep_p,
    keep_q,
    keep_y,
    send_d,
    send_m,
    send_b,
    first_d,
    first_b,
    got_d,
    got_b,
    got_link,
    got_x,
    before,
    value,
    sent,
    sent_first,
    sent_value,
    come_d,
    come_b,
    come_m,
    come_x,
):
    slabs, order = diag.shape[:2]
    inner = slabs - 1
    half = order // 2
    top, low = slice(0, half), slice(half, order)
    me = lax.axis_index("seg") * runs + lax.axis_index("run")
    depth = total.bit_length() - 1
    strides = [1 << i for i in range(depth)]
    root = me == total - 1
    inside = jnp.logical_not(root)
    even = lax.rem(me, 2) == 0
    odd = jnp.logical_not(even)
    parents = [lax.rem(me + 1, 2 * s) == 0 for s in strides]
    level = sum(jnp.where(parent, 1, 0) for parent in parents)
    span = 1 + sum(jnp.where(parent, s, 0) for s, parent in zip(strides, parents))
    next_above = lax.rem(me + span, 4 * span) == 2 * span - 1
    up = jnp.where(next_above, 1, 0)
    peer_p = jnp.where(next_above, me + span, me - span)
    peer_q = jnp.where(next_above, me - span, me + span)
    has_q = jnp.logical_and(inside, jnp.logical_and(peer_q >= 0, peer_q < total))
    slot_p = 1 + 2 * level + (1 - up)
    slot_q = 1 + 2 * level + up

    def copy(source_ref, target_ref, send_sem, recv_sem, peer):
        return pltpu.make_async_remote_copy(
            src_ref=source_ref,
            dst_ref=target_ref,
            send_sem=send_sem,
            recv_sem=recv_sem,
            device_id=(lax.rem(peer, runs), lax.div(peer, runs)),
            device_id_type=MESH,
        )

    barrier = pltpu.get_barrier_semaphore()
    met = [lax.rem(me + 1, s) == 0 for s in strides]
    peers = sum(
        jnp.where(jnp.logical_and(here, ok), 1, 0)
        for s, here in zip(strides, met)
        for ok in (me >= s, me + s < total)
    )
    for s, here in zip(strides, met):
        for ok, peer in ((me >= s, me - s), (me + s < total, me + s)):

            @pl.when(jnp.logical_and(here, ok))
            def _():
                pl.semaphore_signal(
                    barrier,
                    inc=1,
                    device_id=(lax.rem(peer, runs), lax.div(peer, runs)),
                    device_id_type=MESH,
                )

    def first_head(peer):
        return copy(first_d.at[0], got_d.at[0, 0], sent_first.at[0], come_d.at[0], peer)

    def first_tail(peer):
        return copy(
            first_d.at[pl.ds(1, 2)], got_d.at[0, pl.ds(1, 2)], sent_first.at[1], come_d.at[1], peer
        )

    def first_link(peer):
        return copy(send_m, got_link.at[1], sent_first.at[2], come_m.at[1], peer)

    def first_thin(peer):
        return copy(first_b, got_b.at[0], sent_first.at[3], come_b.at[0], peer)

    def head(role, slot, peer):
        return copy(
            send_d.at[role, 0], got_d.at[slot, 0], sent.at[role], come_d.at[2 * slot], peer
        )

    def tail(role, slot, peer):
        return copy(
            send_d.at[role, pl.ds(1, 2)],
            got_d.at[slot, pl.ds(1, 2)],
            sent.at[2 + role],
            come_d.at[2 * slot + 1],
            peer,
        )

    def thin(role, slot, peer):
        return copy(send_b.at[role], got_b.at[slot], sent.at[4 + role], come_b.at[slot], peer)

    def coupled(side, peer):
        return copy(send_m, got_link.at[side], sent.at[6], come_m.at[side], peer)

    def each_source(act):
        @pl.when(inside)
        def _():
            act(0, me + 1)

        for i, s in enumerate(strides):
            for way, (ok, peer) in enumerate(((me >= s, me - s), (me + s < total, me + s))):

                @pl.when(jnp.logical_and(parents[i], ok))
                def _():
                    act(1 + 2 * i + way, peer)

    e_turned[...] = jnp.where(me == 0, jnp.zeros_like(coup[0]), coup[0]).T
    node[0] = diag[0, top, top]
    node[1] = diag[0, top, low]
    node[2] = diag[0, low, low]
    source[...] = rhs[0]
    for i in range(inner):
        final = i == inner - 1
        f_turned = coup.at[i + 1]
        invert(node, x, tile, work, lambda: None)
        w_p[...] = dot(e_turned[...], x[...])

        def put(block, rows, columns):
            term = dot_nt(w_p[rows, :], e_turned[columns, :])
            first_d[block] = -term if i == 0 else first_d[block] - term

        put(0, top, top)
        if final:
            pl.semaphore_wait(barrier, peers)

            @pl.when(me > 0)
            def _():
                first_head(me - 1).start()

        put(1, top, low)
        put(2, low, low)
        if final:

            @pl.when(me > 0)
            def _():
                first_tail(me - 1).start()

        w_q[...] = dot(f_turned[...], x[...])
        node[0] = diag[i + 1, top, top] - dot_nt(w_q[top, :], f_turned[top, :])
        node[1] = diag[i + 1, top, low] - dot_nt(w_q[top, :], f_turned[low, :])
        node[2] = diag[i + 1, low, low] - dot_nt(w_q[low, :], f_turned[low, :])
        if final:

            @pl.when(odd)
            def _():
                send_m[...] = -dot_nt(w_q[...], e_turned[...])
                first_link(me - 1).start()

            @pl.when(even)
            def _():
                got_link[0] = -dot_nt(w_p[...], f_turned[...])

        keep_y[i] = dot(x[...], source[...])
        term = dot(e_turned[...], keep_y[i])
        first_b[...] = -term if i == 0 else first_b[...] - term
        if final:

            @pl.when(me > 0)
            def _():
                first_thin(me - 1).start()

        source[...] = rhs[i + 1] - dot(f_turned[...], keep_y[i])
        keep_p[i] = dot_nt(x[...], e_turned[...])
        keep_q[i] = dot_nt(x[...], f_turned[...])
        if not final:
            e_turned[...] = -dot_nt(w_p[...], f_turned[...])

    def add_head(slot, peer):
        head(0, slot, peer).wait_recv()
        node[0] = node[0] + got_d[slot, 0]

    def add_tail(slot, peer):
        tail(0, slot, peer).wait_recv()
        node[1] = node[1] + got_d[slot, 1]
        node[2] = node[2] + got_d[slot, 2]

    def add_thin(slot, peer):
        thin(0, slot, peer).wait_recv()
        source[...] = source[...] + got_b[slot]

    each_source(add_head)
    invert(node, x, tile, work, lambda: each_source(add_tail))

    @pl.when(inside)
    def _():
        coupled(1, me + 1).wait_recv()

        @pl.when(odd)
        def _():
            coupled(0, me - 1).wait_recv()
            first_link(me - 1).wait_send()

        def serve(role, slot, peer, weights, turned):
            weights[top, :] = dot(turned[top, :], x[...])
            send_d[role, 0] = -dot_nt(weights[top, :], turned[top, :])
            go = inside if role == 0 else has_q

            @pl.when(go)
            def _():
                head(role, slot, peer).start()

            send_d[role, 1] = -dot_nt(weights[top, :], turned[low, :])
            weights[low, :] = dot(turned[low, :], x[...])
            send_d[role, 2] = -dot_nt(weights[low, :], turned[low, :])

            @pl.when(go)
            def _():
                tail(role, slot, peer).start()

        serve(0, slot_p, peer_p, w_p, got_link.at[up])
        serve(1, slot_q, peer_q, w_q, got_link.at[1 - up])

        @pl.when(peer_p < total - 1)
        def _():
            send_m[...] = -dot_nt(w_q[...], got_link[up])
            coupled(1 - up, peer_p).start()

    each_source(add_thin)
    keep_y[inner] = dot(x[...], source[...])
    value[...] = keep_y[inner]

    @pl.when(inside)
    def _():
        send_b[0] = -dot(got_link[up], keep_y[inner])
        thin(0, slot_p, peer_p).start()

        @pl.when(has_q)
        def _():
            send_b[1] = -dot(got_link[1 - up], keep_y[inner])
            thin(1, slot_q, peer_q).start()

        keep_p[inner] = dot_nt(x[...], got_link[up])
        keep_q[inner] = dot_nt(x[...], got_link[1 - up])

        @pl.when(has_q)
        def _():
            copy(value, got_x.at[1], sent_value.at[0], come_x.at[1], peer_q).wait_recv()
            value[...] = value[...] - dot(keep_q[inner], got_x[1])

        copy(value, got_x.at[0], sent_value.at[0], come_x.at[0], peer_p).wait_recv()
        value[...] = value[...] - dot(keep_p[inner], got_x[0])

    def hand_down(act):
        for i, s in reversed(list(enumerate(strides))):
            role = jnp.where(level == i + 1, 0, 1)
            for way, (ok, peer) in enumerate(((me >= s, me - s), (me + s < total, me + s))):

                @pl.when(jnp.logical_and(parents[i], ok))
                def _():
                    act(
                        copy(
                            value, got_x.at[role], sent_value.at[2 * i + way], come_x.at[role], peer
                        )
                    )

        @pl.when(even)
        def _():
            act(copy(value, before, sent_value.at[2 * depth], come_x.at[2], me + 1))

    hand_down(lambda c: c.start())
    out[inner] = value[...]
    for i in reversed(range(inner)):
        out[i] = keep_y[i] - dot(keep_q[i], out[i + 1])

    @pl.when(jnp.logical_and(even, me > 0))
    def _():
        for i in reversed(range(inner)):
            out[i] = out[i] - dot(keep_p[i], got_x[up])

    @pl.when(odd)
    def _():
        copy(value, before, sent_value.at[2 * depth], come_x.at[2], me - 1).wait_recv()
        for i in reversed(range(inner)):
            out[i] = out[i] - dot(keep_p[i], before[...])

    @pl.when(inside)
    def _():
        head(0, slot_p, peer_p).wait_send()
        tail(0, slot_p, peer_p).wait_send()
        thin(0, slot_p, peer_p).wait_send()

        @pl.when(peer_p < total - 1)
        def _():
            coupled(1 - up, peer_p).wait_send()

        @pl.when(has_q)
        def _():
            head(1, slot_q, peer_q).wait_send()
            tail(1, slot_q, peer_q).wait_send()
            thin(1, slot_q, peer_q).wait_send()

    hand_down(lambda c: c.wait_send())

    @pl.when(me > 0)
    def _():
        first_head(me - 1).wait_send()
        first_tail(me - 1).wait_send()
        first_thin(me - 1).wait_send()

    @pl.when(jnp.logical_and(odd, root))
    def _():
        first_link(me - 1).wait_send()


def local(runs, total, diag_blocks, coupling, rhs):
    slabs, order = diag_blocks.shape[1:3]
    half = order // 2
    columns = rhs.shape[3]
    depth = total.bit_length() - 1
    square, thin = (order, order), (order, columns)
    vmem = lambda *shape: pltpu.VMEM(shape, jnp.float32)
    dma = lambda n: pltpu.SemaphoreType.DMA((n,))
    slots = 1 + 2 * depth
    result = pl.pallas_call(
        functools.partial(kernel, runs, total),
        out_shape=jax.ShapeDtypeStruct(rhs.shape[1:], jnp.float32),
        in_specs=[pl.BlockSpec(memory_space=pltpu.VMEM)] * 3,
        out_specs=pl.BlockSpec(memory_space=pltpu.VMEM),
        scratch_shapes=[
            vmem(*square),
            vmem(half, half),
            vmem(2, half, half),
            vmem(3, half, half),
            vmem(*thin),
            vmem(*square),
            vmem(*square),
            vmem(*square),
            vmem(slabs, *square),
            vmem(slabs, *square),
            vmem(slabs, *thin),
            vmem(2, 3, half, half),
            vmem(*square),
            vmem(2, *thin),
            vmem(3, half, half),
            vmem(*thin),
            vmem(slots, 3, half, half),
            vmem(slots, *thin),
            vmem(2, *square),
            vmem(2, *thin),
            vmem(*thin),
            vmem(*thin),
            dma(7),
            dma(4),
            dma(slots),
            dma(2 * slots),
            dma(slots),
            dma(2),
            dma(3),
        ],
        compiler_params=pltpu.CompilerParams(collective_id=0, has_side_effects=True),
        name="chain_solve",
    )(diag_blocks[0], coupling[0], rhs[0])
    return result[None]


def solution(mesh):
    spec = P("seg", "run", None, None)
    runs = mesh.shape["run"]
    total = runs * mesh.shape["seg"]
    return jax.shard_map(
        functools.partial(local, runs, total),
        mesh=mesh,
        in_specs=(spec, spec, spec),
        out_specs=spec,
        check_vma=False,
    )
```

```python
import functools

import jax
import jax.numpy as jnp
from jax import lax
from jax.experimental import pallas as pl
from jax.experimental.pallas import tpu as pltpu
from jax.sharding import PartitionSpec as P

MESH = pl.DeviceIdType.MESH
HIGH = lax.Precision.HIGHEST
ROWS = 8
GROUPS = 2
PIECES = 4
LANES = 128


def dot(a, b):
    return jnp.dot(a, b, precision=HIGH, preferred_element_type=jnp.float32)


def dot_nt(a, b):
    return lax.dot_general(
        a, b, (((1,), (1,)), ((), ())), precision=HIGH, preferred_element_type=jnp.float32
    )


def spread(x, shape):
    return jnp.broadcast_to(x, shape)


def total_of(terms):
    while len(terms) > 1:
        pairs = [terms[t] + terms[t + 1] for t in range(0, len(terms) - 1, 2)]
        terms = pairs + terms[len(pairs) * 2 :]
    return terms[0]


def three_parts(x):
    high = x.astype(jnp.bfloat16)
    rest = x - high.astype(jnp.float32)
    mid = rest.astype(jnp.bfloat16)
    low = (rest - mid.astype(jnp.float32)).astype(jnp.bfloat16)
    return [part.astype(jnp.float32) for part in (high, mid, low)]


def outer_product(left, right):
    lefts = list(zip(*[three_parts(x) for x in left]))
    rights = list(zip(*[three_parts(x) for x in right]))
    order = ((0, 0), (0, 1), (1, 0), (1, 1), (0, 2), (2, 0))
    stack = lambda parts, side: jnp.concatenate(
        [x for pair in order for x in parts[pair[side]]], axis=0
    ).astype(jnp.bfloat16)
    return lax.dot_general(
        stack(lefts, 0),
        stack(rights, 1),
        (((0,), (0,)), ((), ())),
        preferred_element_type=jnp.float32,
    )


def eliminate_panel(panel, first, sub, lane):
    shape = panel[0].shape
    groups = len(panel)
    width = groups * ROWS
    cols = [
        [jnp.where(lane >= 0, spread(p[:, first + j : first + j + 1], shape), 0.0) for p in panel]
        for j in range(width)
    ]
    for j in range(width):
        own, row = divmod(j, ROWS)
        here = sub == row
        inverse = 1.0 / spread(cols[j][own][row : row + 1, :], shape)
        factor = [jnp.where(here, -1.0, c) if i == own else c for i, c in enumerate(cols[j])]
        scaled = [f * inverse for f in factor]
        clear = lambda x, i: jnp.where(here, 0.0, x) if i == own else x
        for m in range(j + 1, width):
            line = spread(cols[m][own][row : row + 1, :], shape)
            if m == j + 1:
                steps = [(f * line) * inverse for f in factor]
            else:
                steps = [s * line for s in scaled]
            cols[m] = [clear(c, i) - steps[i] for i, c in enumerate(cols[m])]
        at = lane == first + j
        line = jnp.where(at, 1.0, spread(panel[own][row : row + 1, :], shape))
        panel = [
            clear(jnp.where(at, 0.0, p), i) - scaled[i] * line for i, p in enumerate(panel)
        ]
    return panel


def spd_inverse_tile(rows):
    shape = rows[0].shape
    sub = lax.broadcasted_iota(jnp.int32, shape, 0)
    lane = lax.broadcasted_iota(jnp.int32, shape, 1)
    rows = list(rows)
    width = GROUPS * ROWS
    for k in range(0, len(rows), GROUPS):
        first = k * ROWS
        inside = jnp.logical_and(lane >= first, lane < first + width)
        panel = rows[k : k + GROUPS]
        columns = [
            jnp.where(lane < first, -p, jnp.where(inside, 0.0, p)) for p in panel
        ]
        panel = eliminate_panel(panel, first, sub, lane)
        near = range(k + GROUPS, min(k + 2 * GROUPS, len(rows)))
        for i in near:
            terms = [
                spread(rows[i][:, first + j : first + j + 1], shape)
                * spread(panel[j // ROWS][j % ROWS : j % ROWS + 1, :], shape)
                for j in range(width)
            ]
            rows[i] = jnp.where(inside, 0.0, rows[i]) - total_of(terms)
        update = outer_product(columns, panel)
        for i in range(len(rows)):
            if i < k or i >= k + 2 * GROUPS:
                rows[i] = jnp.where(inside, 0.0, rows[i]) - update[i * ROWS : (i + 1) * ROWS, :]
        rows[k : k + GROUPS] = panel
    return rows


def invert(node, x, tile, work, late):
    half = tile.shape[0]
    top, low = slice(0, half), slice(half, 2 * half)
    tile[...] = node[0]

    @pl.loop(0, 2)
    def _(step):
        rows = spd_inverse_tile([tile[i : i + ROWS, :] for i in range(0, half, ROWS)])
        for i, row in enumerate(rows):
            tile[i * ROWS : (i + 1) * ROWS, :] = row

        @pl.when(step == 0)
        def _():
            late()
            x[top, top] = tile[...]
            work[0] = dot(tile[...], node[1])
            work[1] = work[0].T
            tile[...] = node[2] - dot(work[1], node[1])

        @pl.when(step == 1)
        def _():
            corner = -dot(tile[...], work[1])
            x[low, low] = tile[...]
            x[low, top] = corner
            x[top, low] = -dot(work[0], tile[...])
            x[top, top] = x[top, top] - dot(work[0], corner)


def kernel(
    runs,
    total,
    diag,
    coup,
    rhs,
    out,
    x,
    tile,
    work,
    node,
    source,
    e_turned,
    w_p,
    w_q,
    keep_p,
    keep_q,
    keep_y,
    send_d,
    send_m,
    send_b,
    first_d,
    first_b,
    got_d,
    got_b,
    got_link,
    got_x,
    before,
    value,
    passing,
    sent,
    sent_first,
    sent_value,
    sent_pass,
    come_d,
    come_b,
    come_m,
    come_x,
    come_pass,
):
    slabs, order = diag.shape[:2]
    inner = slabs - 1
    half = order // 2
    top, low = slice(0, half), slice(half, order)
    me = lax.axis_index("seg") * runs + lax.axis_index("run")
    depth = total.bit_length() - 1
    strides = [1 << i for i in range(depth)]
    root = me == total - 1
    inside = jnp.logical_not(root)
    even = lax.rem(me, 2) == 0
    odd = jnp.logical_not(even)
    parents = [lax.rem(me + 1, 2 * s) == 0 for s in strides]
    level = sum(jnp.where(parent, 1, 0) for parent in parents)
    span = 1 + sum(jnp.where(parent, s, 0) for s, parent in zip(strides, parents))
    next_above = lax.rem(me + span, 4 * span) == 2 * span - 1
    up = jnp.where(next_above, 1, 0)
    peer_p = jnp.where(next_above, me + span, me - span)
    peer_q = jnp.where(next_above, me - span, me + span)
    has_q = jnp.logical_and(inside, jnp.logical_and(peer_q >= 0, peer_q < total))
    slot_p = 1 + 2 * level + (1 - up)
    slot_q = 1 + 2 * level + up
    bends = bend_strides(runs, total)
    piece = order // PIECES

    def copy(source_ref, target_ref, send_sem, recv_sem, peer):
        return pltpu.make_async_remote_copy(
            src_ref=source_ref,
            dst_ref=target_ref,
            send_sem=send_sem,
            recv_sem=recv_sem,
            device_id=(lax.rem(peer, runs), lax.div(peer, runs)),
            device_id_type=MESH,
        )

    barrier = pltpu.get_barrier_semaphore()
    met = [lax.rem(me + 1, s) == 0 for s in strides]
    greeted = [
        (jnp.logical_and(here, ok), peer)
        for s, here in zip(strides, met)
        for ok, peer in ((me >= s, me - s), (me + s < total, me + s))
    ]
    for s in bends:
        greeted.append((lax.rem(me + 1, 4 * s) == 3 * s, me + s - 1))
        greeted.append((lax.rem(me + 2, 4 * s) == 0, me + 1 - s))
        greeted.append((lax.rem(me + 2, 4 * s) == 0, me + 1 - 2 * s))
        greeted.append((lax.rem(me + 1, 4 * s) == 2 * s, me + 2 * s - 1))
    peers = sum(jnp.where(ok, 1, 0) for ok, _ in greeted)
    for ok, peer in greeted:

        @pl.when(ok)
        def _():
            pl.semaphore_signal(
                barrier,
                inc=1,
                device_id=(lax.rem(peer, runs), lax.div(peer, runs)),
                device_id_type=MESH,
            )

    def first_head(peer):
        return copy(first_d.at[0], got_d.at[0, 0], sent_first.at[0], come_d.at[0], peer)

    def first_tail(peer):
        return copy(
            first_d.at[pl.ds(1, 2)], got_d.at[0, pl.ds(1, 2)], sent_first.at[1], come_d.at[1], peer
        )

    def first_link(peer):
        return copy(send_m, got_link.at[1], sent_first.at[2], come_m.at[1], peer)

    def first_thin(peer):
        return copy(first_b, got_b.at[0], sent_first.at[3], come_b.at[0], peer)

    def head(role, slot, peer):
        return copy(
            send_d.at[role, 0], got_d.at[slot, 0], sent.at[role], come_d.at[2 * slot], peer
        )

    def tail(role, slot, peer):
        return copy(
            send_d.at[role, pl.ds(1, 2)],
            got_d.at[slot, pl.ds(1, 2)],
            sent.at[2 + role],
            come_d.at[2 * slot + 1],
            peer,
        )

    def thin(role, slot, peer):
        return copy(send_b.at[role], got_b.at[slot], sent.at[4 + role], come_b.at[slot], peer)

    def coupled(side, peer):
        return copy(send_m, got_link.at[side], sent.at[6], come_m.at[side], peer)

    def to_bend(which, part, peer):
        rows = pl.ds(part * piece, piece)
        return copy(
            send_m.at[rows],
            passing.at[which, rows],
            sent.at[6],
            come_pass.at[which * PIECES + part],
            peer,
        )

    def from_bend(which, part, peer):
        rows = pl.ds(part * piece, piece)
        return copy(
            passing.at[which, rows],
            got_link.at[1, rows],
            sent_pass.at[which * PIECES + part],
            come_m.at[1],
            peer,
        )

    def each_source(act):
        @pl.when(inside)
        def _():
            act(0, me + 1)

        for i, s in enumerate(strides):
            for way, (ok, peer) in enumerate(((me >= s, me - s), (me + s < total, me + s))):

                @pl.when(jnp.logical_and(parents[i], ok))
                def _():
                    act(1 + 2 * i + way, peer)

    e_turned[...] = jnp.where(me == 0, jnp.zeros_like(coup[0]), coup[0]).T
    node[0] = diag[0, top, top]
    node[1] = diag[0, top, low]
    node[2] = diag[0, low, low]
    source[...] = rhs[0]
    for i in range(inner):
        final = i == inner - 1
        f_turned = coup.at[i + 1]
        invert(node, x, tile, work, lambda: None)
        w_p[...] = dot(e_turned[...], x[...])

        def put(block, rows, columns):
            term = dot_nt(w_p[rows, :], e_turned[columns, :])
            first_d[block] = -term if i == 0 else first_d[block] - term

        put(0, top, top)
        if final:
            pl.semaphore_wait(barrier, peers)

            @pl.when(me > 0)
            def _():
                first_head(me - 1).start()

        put(1, top, low)
        put(2, low, low)
        if final:

            @pl.when(me > 0)
            def _():
                first_tail(me - 1).start()

        w_q[...] = dot(f_turned[...], x[...])
        node[0] = diag[i + 1, top, top] - dot_nt(w_q[top, :], f_turned[top, :])
        node[1] = diag[i + 1, top, low] - dot_nt(w_q[top, :], f_turned[low, :])
        node[2] = diag[i + 1, low, low] - dot_nt(w_q[low, :], f_turned[low, :])
        if final:

            @pl.when(odd)
            def _():
                send_m[...] = -dot_nt(w_q[...], e_turned[...])
                first_link(me - 1).start()

            @pl.when(even)
            def _():
                got_link[0] = -dot_nt(w_p[...], f_turned[...])

        keep_y[i] = dot(x[...], source[...])
        term = dot(e_turned[...], keep_y[i])
        first_b[...] = -term if i == 0 else first_b[...] - term
        if final:

            @pl.when(me > 0)
            def _():
                first_thin(me - 1).start()

        source[...] = rhs[i + 1] - dot(f_turned[...], keep_y[i])
        keep_p[i] = dot_nt(x[...], e_turned[...])
        keep_q[i] = dot_nt(x[...], f_turned[...])
        if not final:
            e_turned[...] = -dot_nt(w_p[...], f_turned[...])

    def add_head(slot, peer):
        head(0, slot, peer).wait_recv()
        node[0] = node[0] + got_d[slot, 0]

    def add_tail(slot, peer):
        tail(0, slot, peer).wait_recv()
        node[1] = node[1] + got_d[slot, 1]
        node[2] = node[2] + got_d[slot, 2]

    def add_thin(slot, peer):
        thin(0, slot, peer).wait_recv()
        source[...] = source[...] + got_b[slot]

    each_source(add_head)
    invert(node, x, tile, work, lambda: each_source(add_tail))

    def serve(role, slot, peer, weights, turned):
        weights[top, :] = dot(turned[top, :], x[...])
        send_d[role, 0] = -dot_nt(weights[top, :], turned[top, :])
        go = inside if role == 0 else has_q

        @pl.when(go)
        def _():
            head(role, slot, peer).start()

        send_d[role, 1] = -dot_nt(weights[top, :], turned[low, :])
        weights[low, :] = dot(turned[low, :], x[...])
        send_d[role, 2] = -dot_nt(weights[low, :], turned[low, :])

        @pl.when(go)
        def _():
            tail(role, slot, peer).start()

    @pl.when(inside)
    def _():
        coupled(1, me + 1).wait_recv()

        @pl.when(odd)
        def _():
            coupled(0, me - 1).wait_recv()
            first_link(me - 1).wait_send()

        serve(0, slot_p, peer_p, w_p, got_link.at[up])

        @pl.when(peer_p < total - 1)
        def _():
            send_m[...] = -dot_nt(got_link[1 - up], w_p[...])
            bent = [lax.rem(me + 1, 4 * s) == 3 * s for s in bends]
            for i, s in enumerate(bends):

                @pl.when(bent[i])
                def _():
                    for part in range(PIECES):
                        to_bend(i, part, me + s - 1).start()

            straight = sum(jnp.where(b, 1, 0) for b in bent) == 0

            @pl.when(straight)
            def _():
                coupled(1 - up, peer_p).start()

        keep_p[inner] = dot_nt(x[...], got_link[up])
        keep_q[inner] = dot_nt(x[...], got_link[1 - up])

    each_source(add_thin)
    keep_y[inner] = dot(x[...], source[...])
    value[...] = keep_y[inner]

    @pl.when(inside)
    def _():
        send_b[0] = -dot(got_link[up], keep_y[inner])
        thin(0, slot_p, peer_p).start()
        serve(1, slot_q, peer_q, w_q, got_link.at[1 - up])

        @pl.when(has_q)
        def _():
            send_b[1] = -dot(got_link[1 - up], keep_y[inner])
            thin(1, slot_q, peer_q).start()

        for i, s in enumerate(bends):

            @pl.when(lax.rem(me + 2, 4 * s) == 0)
            def _():
                for part in range(PIECES):
                    to_bend(i, part, me).wait_recv()
                    from_bend(i, part, me + 1 - 2 * s).start()

        @pl.when(has_q)
        def _():
            copy(value, got_x.at[1], sent_value.at[0], come_x.at[1], peer_q).wait_recv()
            value[...] = value[...] - dot(keep_q[inner], got_x[1])

        copy(value, got_x.at[0], sent_value.at[0], come_x.at[0], peer_p).wait_recv()
        value[...] = value[...] - dot(keep_p[inner], got_x[0])

    def hand_down(act):
        for i, s in reversed(list(enumerate(strides))):
            role = jnp.where(level == i + 1, 0, 1)
            for way, (ok, peer) in enumerate(((me >= s, me - s), (me + s < total, me + s))):

                @pl.when(jnp.logical_and(parents[i], ok))
                def _():
                    act(
                        copy(
                            value, got_x.at[role], sent_value.at[2 * i + way], come_x.at[role], peer
                        )
                    )

        @pl.when(even)
        def _():
            act(copy(value, before, sent_value.at[2 * depth], come_x.at[2], me + 1))

    hand_down(lambda c: c.start())
    out[inner] = value[...]
    for i in reversed(range(inner)):
        out[i] = keep_y[i] - dot(keep_q[i], out[i + 1])

    @pl.when(jnp.logical_and(even, me > 0))
    def _():
        for i in reversed(range(inner)):
            out[i] = out[i] - dot(keep_p[i], got_x[up])

    @pl.when(odd)
    def _():
        copy(value, before, sent_value.at[2 * depth], come_x.at[2], me - 1).wait_recv()
        for i in reversed(range(inner)):
            out[i] = out[i] - dot(keep_p[i], before[...])

    @pl.when(inside)
    def _():
        head(0, slot_p, peer_p).wait_send()
        tail(0, slot_p, peer_p).wait_send()
        thin(0, slot_p, peer_p).wait_send()

        @pl.when(peer_p < total - 1)
        def _():
            coupled(1 - up, peer_p).wait_send()

        @pl.when(has_q)
        def _():
            head(1, slot_q, peer_q).wait_send()
            tail(1, slot_q, peer_q).wait_send()
            thin(1, slot_q, peer_q).wait_send()

    hand_down(lambda c: c.wait_send())
    for i, s in enumerate(bends):

        @pl.when(lax.rem(me + 2, 4 * s) == 0)
        def _():
            for part in range(PIECES):
                from_bend(i, part, me + 1 - 2 * s).wait_send()

    @pl.when(me > 0)
    def _():
        first_head(me - 1).wait_send()
        first_tail(me - 1).wait_send()
        first_thin(me - 1).wait_send()

    @pl.when(jnp.logical_and(odd, root))
    def _():
        first_link(me - 1).wait_send()


def bend_strides(runs, total):
    stride = runs // 2
    return [stride] if stride > 1 and 4 * stride <= total else []


def local(runs, total, diag_blocks, coupling, rhs):
    slabs, order = diag_blocks.shape[1:3]
    half = order // 2
    columns = rhs.shape[3]
    depth = total.bit_length() - 1
    square, thin = (order, order), (order, columns)
    vmem = lambda *shape: pltpu.VMEM(shape, jnp.float32)
    dma = lambda n: pltpu.SemaphoreType.DMA((n,))
    slots = 1 + 2 * depth
    bends = len(bend_strides(runs, total))
    result = pl.pallas_call(
        functools.partial(kernel, runs, total),
        out_shape=jax.ShapeDtypeStruct(rhs.shape[1:], jnp.float32),
        in_specs=[pl.BlockSpec(memory_space=pltpu.VMEM)] * 3,
        out_specs=pl.BlockSpec(memory_space=pltpu.VMEM),
        scratch_shapes=[
            vmem(*square),
            vmem(half, half),
            vmem(2, half, half),
            vmem(3, half, half),
            vmem(*thin),
            vmem(*square),
            vmem(*square),
            vmem(*square),
            vmem(slabs, *square),
            vmem(slabs, *square),
            vmem(slabs, *thin),
            vmem(2, 3, half, half),
            vmem(*square),
            vmem(2, *thin),
            vmem(3, half, half),
            vmem(*thin),
            vmem(slots, 3, half, half),
            vmem(slots, *thin),
            vmem(2, *square),
            vmem(2, *thin),
            vmem(*thin),
            vmem(*thin),
            vmem(bends, *square),
            dma(7),
            dma(4),
            dma(slots),
            dma(bends * PIECES),
            dma(2 * slots),
            dma(slots),
            dma(2),
            dma(3),
            dma(bends * PIECES),
        ],
        compiler_params=pltpu.CompilerParams(collective_id=0, has_side_effects=True),
        name="chain_solve",
    )(diag_blocks[0], coupling[0], rhs[0])
    return result[None]


def solution(mesh):
    spec = P("seg", "run", None, None)
    runs = mesh.shape["run"]
    total = runs * mesh.shape["seg"]
    return jax.shard_map(
        functools.partial(local, runs, total),
        mesh=mesh,
        in_specs=(spec, spec, spec),
        out_specs=spec,
        check_vma=False,
    )
```

```python
import functools

import jax
import jax.numpy as jnp
from jax import lax
from jax.experimental import pallas as pl
from jax.experimental.pallas import tpu as pltpu
from jax.sharding import PartitionSpec as P

MESH = pl.DeviceIdType.MESH
HIGH = lax.Precision.HIGHEST
ROWS = 8
GROUPS = 2
PIECES = 4
LANES = 128


def dot(a, b):
    return jnp.dot(a, b, precision=HIGH, preferred_element_type=jnp.float32)


def dot_nt(a, b):
    return lax.dot_general(
        a, b, (((1,), (1,)), ((), ())), precision=HIGH, preferred_element_type=jnp.float32
    )


def spread(x, shape):
    return jnp.broadcast_to(x, shape)


def total_of(terms):
    while len(terms) > 1:
        pairs = [terms[t] + terms[t + 1] for t in range(0, len(terms) - 1, 2)]
        terms = pairs + terms[len(pairs) * 2 :]
    return terms[0]


def three_parts(x):
    high = x.astype(jnp.bfloat16)
    rest = x - high.astype(jnp.float32)
    mid = rest.astype(jnp.bfloat16)
    low = (rest - mid.astype(jnp.float32)).astype(jnp.bfloat16)
    return [part.astype(jnp.float32) for part in (high, mid, low)]


def outer_product(left, right):
    lefts = list(zip(*[three_parts(x) for x in left]))
    rights = list(zip(*[three_parts(x) for x in right]))
    order = ((0, 0), (0, 1), (1, 0), (1, 1), (0, 2), (2, 0))
    stack = lambda parts, side: jnp.concatenate(
        [x for pair in order for x in parts[pair[side]]], axis=0
    ).astype(jnp.bfloat16)
    return lax.dot_general(
        stack(lefts, 0),
        stack(rights, 1),
        (((0,), (0,)), ((), ())),
        preferred_element_type=jnp.float32,
    )


def eliminate_panel(panel, first, sub, lane):
    shape = panel[0].shape
    groups = len(panel)
    width = groups * ROWS
    cols = [[spread(p[:, first + j : first + j + 1], shape) for p in panel] for j in range(width)]
    for col in cols:
        col[0] = jnp.where(lane >= 0, col[0], 0.0)
    inverses = [jnp.zeros(shape, jnp.float32)] * groups
    for j in range(width):
        own, row = divmod(j, ROWS)
        here = sub == row
        inverse = 1.0 / spread(cols[j][own][row : row + 1, :], shape)
        inverses[own] = jnp.where(here, inverse, inverses[own])
        factor = [jnp.where(here, 0.0, c) if i == own else c for i, c in enumerate(cols[j])]
        scaled = [f * inverse for f in factor]
        for m in range(j + 1, width):
            line = spread(cols[m][own][row : row + 1, :], shape)
            if m == j + 1:
                steps = [(f * line) * inverse for f in factor]
            else:
                steps = [f * line for f in scaled]
            cols[m] = [c - step for c, step in zip(cols[m], steps)]
        at = lane == first + j
        line = jnp.where(at, 1.0, spread(panel[own][row : row + 1, :], shape))
        unit = jnp.where(here, 1.0, 0.0)
        panel = [
            jnp.where(at, unit if i == own else 0.0, p) - scaled[i] * line
            for i, p in enumerate(panel)
        ]
    return [p * scale for p, scale in zip(panel, inverses)]


def spd_inverse_tile(rows):
    shape = rows[0].shape
    sub = lax.broadcasted_iota(jnp.int32, shape, 0)
    lane = lax.broadcasted_iota(jnp.int32, shape, 1)
    rows = list(rows)
    width = GROUPS * ROWS
    for k in range(0, len(rows), GROUPS):
        first = k * ROWS
        inside = jnp.logical_and(lane >= first, lane < first + width)
        panel = rows[k : k + GROUPS]
        columns = [
            jnp.where(lane < first, -p, jnp.where(inside, 0.0, p)) for p in panel
        ]
        panel = eliminate_panel(panel, first, sub, lane)
        near = range(k + GROUPS, min(k + 2 * GROUPS, len(rows)))
        for i in near:
            terms = [
                spread(rows[i][:, first + j : first + j + 1], shape)
                * spread(panel[j // ROWS][j % ROWS : j % ROWS + 1, :], shape)
                for j in range(width)
            ]
            rows[i] = jnp.where(inside, 0.0, rows[i]) - total_of(terms)
        update = outer_product(columns, panel)
        for i in range(len(rows)):
            if i < k or i >= k + 2 * GROUPS:
                rows[i] = jnp.where(inside, 0.0, rows[i]) - update[i * ROWS : (i + 1) * ROWS, :]
        rows[k : k + GROUPS] = panel
    return rows


def invert(node, x, tile, work, late):
    half = tile.shape[0]
    top, low = slice(0, half), slice(half, 2 * half)
    tile[...] = node[0]

    @pl.loop(0, 2)
    def _(step):
        rows = spd_inverse_tile([tile[i : i + ROWS, :] for i in range(0, half, ROWS)])
        for i, row in enumerate(rows):
            tile[i * ROWS : (i + 1) * ROWS, :] = row

        @pl.when(step == 0)
        def _():
            late()
            x[top, top] = tile[...]
            work[0] = dot(tile[...], node[1])
            work[1] = work[0].T
            tile[...] = node[2] - dot(work[1], node[1])

        @pl.when(step == 1)
        def _():
            corner = -dot(tile[...], work[1])
            x[low, low] = tile[...]
            x[low, top] = corner
            x[top, low] = -dot(work[0], tile[...])
            x[top, top] = x[top, top] - dot(work[0], corner)


def kernel(
    runs,
    total,
    diag,
    coup,
    rhs,
    out,
    first_x,
    x,
    tile,
    work,
    node,
    source,
    e_turned,
    w_p,
    w_q,
    keep_p,
    keep_q,
    keep_y,
    send_d,
    send_m,
    send_t,
    send_b,
    first_d,
    first_b,
    got_d,
    got_b,
    got_link,
    got_x,
    before,
    value,
    passing,
    sent,
    sent_first,
    sent_value,
    sent_pass,
    come_d,
    come_b,
    come_m,
    come_x,
    come_pass,
):
    slabs, order = diag.shape[:2]
    inner = slabs - 1
    half = order // 2
    top, low = slice(0, half), slice(half, order)
    me = lax.axis_index("seg") * runs + lax.axis_index("run")
    depth = total.bit_length() - 1
    strides = [1 << i for i in range(depth)]
    last = me == total - 1
    inside = jnp.logical_not(last)
    pair = lax.rem(me + 1, total // 2) == 0
    single = jnp.logical_not(pair)
    tells_last = me == total - 1 - total // 4
    even = lax.rem(me, 2) == 0
    odd = jnp.logical_not(even)
    steps = strides[:-1]
    parents = [lax.rem(me + 1, 2 * s) == 0 for s in steps]
    level = sum(jnp.where(parent, 1, 0) for parent in parents)
    span = 1 + sum(jnp.where(parent, s, 0) for s, parent in zip(steps, parents))
    next_above = lax.rem(me + span, 4 * span) == 2 * span - 1
    up = jnp.where(next_above, 1, 0)
    peer_p = jnp.where(next_above, me + span, me - span)
    peer_q = jnp.where(next_above, me - span, me + span)
    has_q = jnp.logical_and(peer_q >= 0, peer_q < total)
    slot_p = 1 + 2 * level + (1 - up)
    slot_q = 1 + 2 * level + up
    bends = bend_strides(runs, total)
    piece = order // PIECES

    def copy(source_ref, target_ref, send_sem, recv_sem, peer):
        return pltpu.make_async_remote_copy(
            src_ref=source_ref,
            dst_ref=target_ref,
            send_sem=send_sem,
            recv_sem=recv_sem,
            device_id=(lax.rem(peer, runs), lax.div(peer, runs)),
            device_id_type=MESH,
        )

    barrier = pltpu.get_barrier_semaphore()
    met = [lax.rem(me + 1, s) == 0 for s in strides]
    greeted = [
        (jnp.logical_and(here, ok), peer)
        for s, here in zip(strides, met)
        for ok, peer in ((me >= s, me - s), (me + s < total, me + s))
    ]
    for s in bends:
        greeted.append((lax.rem(me + 1, 4 * s) == 3 * s, me + s - 1))
        greeted.append((lax.rem(me + 2, 4 * s) == 0, me + 1 - s))
        greeted.append((lax.rem(me + 2, 4 * s) == 0, me + 1 - 2 * s))
        greeted.append((lax.rem(me + 1, 4 * s) == 2 * s, me + 2 * s - 1))
    peers = sum(jnp.where(ok, 1, 0) for ok, _ in greeted)
    for ok, peer in greeted:

        @pl.when(ok)
        def _():
            pl.semaphore_signal(
                barrier,
                inc=1,
                device_id=(lax.rem(peer, runs), lax.div(peer, runs)),
                device_id_type=MESH,
            )

    def first_head(peer):
        return copy(first_d.at[0], got_d.at[0, 0], sent_first.at[0], come_d.at[0], peer)

    def first_tail(peer):
        return copy(
            first_d.at[pl.ds(1, 2)], got_d.at[0, pl.ds(1, 2)], sent_first.at[1], come_d.at[1], peer
        )

    def first_link(peer):
        return copy(send_m, got_link.at[1], sent_first.at[2], come_m.at[1], peer)

    def first_thin(peer):
        return copy(first_b, got_b.at[0], sent_first.at[3], come_b.at[0], peer)

    def head(role, slot, peer):
        return copy(
            send_d.at[role, 0], got_d.at[slot, 0], sent.at[role], come_d.at[2 * slot], peer
        )

    def tail(role, slot, peer):
        return copy(
            send_d.at[role, pl.ds(1, 2)],
            got_d.at[slot, pl.ds(1, 2)],
            sent.at[2 + role],
            come_d.at[2 * slot + 1],
            peer,
        )

    def thin(role, slot, peer):
        return copy(send_b.at[role], got_b.at[slot], sent.at[4 + role], come_b.at[slot], peer)

    def coupled(side, peer):
        return copy(send_m, got_link.at[side], sent.at[6], come_m.at[side], peer)

    def mirrored():
        return copy(send_t, got_link.at[0], sent.at[7], come_m.at[0], total - 1)

    def to_bend(which, part, peer):
        rows = pl.ds(part * piece, piece)
        return copy(
            send_m.at[rows],
            passing.at[which, rows],
            sent.at[6],
            come_pass.at[which * PIECES + part],
            peer,
        )

    def from_bend(which, part, peer):
        rows = pl.ds(part * piece, piece)
        return copy(
            passing.at[which, rows],
            got_link.at[1, rows],
            sent_pass.at[which * PIECES + part],
            come_m.at[1],
            peer,
        )

    def each_source(act):
        @pl.when(inside)
        def _():
            act(0, me + 1)

        for i, s in enumerate(steps):
            for way, (ok, peer) in enumerate(((me >= s, me - s), (me + s < total, me + s))):

                @pl.when(jnp.logical_and(parents[i], ok))
                def _():
                    act(1 + 2 * i + way, peer)

    e_turned[...] = jnp.where(me == 0, jnp.zeros_like(coup[0]), coup[0]).T
    node[0] = diag[0, top, top]
    node[1] = diag[0, top, low]
    node[2] = diag[0, low, low]
    source[...] = rhs[0]
    for i in range(inner):
        final = i == inner - 1
        f_turned = coup.at[i + 1]
        invert(node, first_x, tile, work, lambda: None)
        w_p[...] = dot(e_turned[...], first_x[...])

        def put(block, rows, columns):
            term = dot_nt(w_p[rows, :], e_turned[columns, :])
            first_d[block] = -term if i == 0 else first_d[block] - term

        put(0, top, top)
        if final:
            pl.semaphore_wait(barrier, peers)

            @pl.when(me > 0)
            def _():
                first_head(me - 1).start()

        put(1, top, low)
        put(2, low, low)
        if final:

            @pl.when(me > 0)
            def _():
                first_tail(me - 1).start()

        w_q[...] = dot(f_turned[...], first_x[...])
        node[0] = diag[i + 1, top, top] - dot_nt(w_q[top, :], f_turned[top, :])
        node[1] = diag[i + 1, top, low] - dot_nt(w_q[top, :], f_turned[low, :])
        node[2] = diag[i + 1, low, low] - dot_nt(w_q[low, :], f_turned[low, :])

        def rest(i):
            f_turned = coup.at[i + 1]
            keep_y[i] = dot(first_x[...], source[...])
            term = dot(e_turned[...], keep_y[i])
            first_b[...] = -term if i == 0 else first_b[...] - term
            if i == inner - 1:

                @pl.when(me > 0)
                def _():
                    first_thin(me - 1).start()

            source[...] = rhs[i + 1] - dot(f_turned[...], keep_y[i])
            keep_p[i] = dot_nt(first_x[...], e_turned[...])
            keep_q[i] = dot_nt(first_x[...], f_turned[...])

        if final:

            @pl.when(odd)
            def _():
                send_m[...] = -dot_nt(w_q[...], e_turned[...])
                first_link(me - 1).start()
                rest(inner - 1)

            @pl.when(even)
            def _():
                got_link[0] = -dot_nt(w_p[...], f_turned[...])

        else:
            rest(i)
            e_turned[...] = -dot_nt(w_p[...], f_turned[...])

    def add_head(slot, peer):
        head(0, slot, peer).wait_recv()
        node[0] = node[0] + got_d[slot, 0]

    def add_tail(slot, peer):
        tail(0, slot, peer).wait_recv()
        node[1] = node[1] + got_d[slot, 1]
        node[2] = node[2] + got_d[slot, 2]

    def add_thin(slot, peer):
        thin(0, slot, peer).wait_recv()
        source[...] = source[...] + got_b[slot]

    each_source(add_head)
    invert(node, x, tile, work, lambda: each_source(add_tail))

    def serve_head(role, slot, peer, weights, turned):
        weights[top, :] = dot(turned[top, :], x[...])
        send_d[role, 0] = -dot_nt(weights[top, :], turned[top, :])
        head(role, slot, peer).start()

    def serve_tail(role, slot, peer, weights, turned):
        send_d[role, 1] = -dot_nt(weights[top, :], turned[low, :])
        weights[low, :] = dot(turned[low, :], x[...])
        send_d[role, 2] = -dot_nt(weights[low, :], turned[low, :])
        tail(role, slot, peer).start()

    @pl.when(inside)
    def _():
        coupled(1, me + 1).wait_recv()

    @pl.when(odd)
    def _():
        coupled(0, me - 1).wait_recv()
        first_link(me - 1).wait_send()

    to_p = (0, slot_p, peer_p, w_p, got_link.at[up])
    to_q = (1, slot_q, peer_q, w_q, got_link.at[1 - up])
    serve_head(*to_p)

    @pl.when(tells_last)
    def _():
        serve_head(*to_q)

    serve_tail(*to_p)

    @pl.when(tells_last)
    def _():
        serve_tail(*to_q)

    @pl.when(single)
    def _():
        send_m[...] = -dot_nt(got_link[1 - up], w_p[...])
        bent = [lax.rem(me + 1, 4 * s) == 3 * s for s in bends]
        for i, s in enumerate(bends):

            @pl.when(bent[i])
            def _():
                for part in range(PIECES):
                    to_bend(i, part, me + s - 1).start()

        straight = sum(jnp.where(b, 1, 0) for b in bent) == 0

        @pl.when(straight)
        def _():
            coupled(1 - up, peer_p).start()

        @pl.when(tells_last)
        def _():
            send_t[...] = -dot_nt(w_p[...], got_link[1 - up])
            mirrored().start()

        keep_p[inner] = dot_nt(x[...], got_link[up])
        keep_q[inner] = dot_nt(x[...], got_link[1 - up])

    @pl.when(even)
    def _():
        rest(inner - 1)

    each_source(add_thin)
    keep_y[inner] = dot(x[...], source[...])
    send_b[0] = -dot(got_link[up], keep_y[inner])
    thin(0, slot_p, peer_p).start()

    @pl.when(has_q)
    def _():

        @pl.when(jnp.logical_not(tells_last))
        def _():
            serve_head(*to_q)
            serve_tail(*to_q)

        send_b[1] = -dot(got_link[1 - up], keep_y[inner])
        thin(1, slot_q, peer_q).start()

    for i, s in enumerate(bends):

        @pl.when(lax.rem(me + 2, 4 * s) == 0)
        def _():
            for part in range(PIECES):
                to_bend(i, part, me).wait_recv()
                from_bend(i, part, me + 1 - 2 * s).start()

    @pl.when(single)
    def _():
        value[...] = keep_y[inner]

        @pl.when(has_q)
        def _():
            copy(value, got_x.at[1], sent_value.at[0], come_x.at[1], peer_q).wait_recv()
            value[...] = value[...] - dot(keep_q[inner], got_x[1])

        copy(value, got_x.at[0], sent_value.at[0], come_x.at[0], peer_p).wait_recv()
        value[...] = value[...] - dot(keep_p[inner], got_x[0])

    @pl.when(pair)
    def _():
        slot = 1 + 2 * level + up
        add_head(slot, peer_p)
        invert(node, x, tile, work, lambda: add_tail(slot, peer_p))
        add_thin(slot, peer_p)
        value[...] = dot(x[...], source[...])

    def hand_down(act):
        for i, s in reversed(list(enumerate(steps))):
            role = jnp.where(jnp.logical_and(level == i + 1, inside), 0, 1)
            for way, (ok, peer) in enumerate(((me >= s, me - s), (me + s < total, me + s))):

                @pl.when(jnp.logical_and(parents[i], ok))
                def _():
                    act(
                        copy(
                            value, got_x.at[role], sent_value.at[2 * i + way], come_x.at[role], peer
                        )
                    )

        @pl.when(even)
        def _():
            act(copy(value, before, sent_value.at[2 * depth], come_x.at[2], me + 1))

    hand_down(lambda c: c.start())
    out[inner] = value[...]
    for i in reversed(range(inner)):
        out[i] = keep_y[i] - dot(keep_q[i], out[i + 1])

    @pl.when(jnp.logical_and(even, me > 0))
    def _():
        for i in reversed(range(inner)):
            out[i] = out[i] - dot(keep_p[i], got_x[up])

    @pl.when(odd)
    def _():
        copy(value, before, sent_value.at[2 * depth], come_x.at[2], me - 1).wait_recv()
        for i in reversed(range(inner)):
            out[i] = out[i] - dot(keep_p[i], before[...])

    head(0, slot_p, peer_p).wait_send()
    tail(0, slot_p, peer_p).wait_send()
    thin(0, slot_p, peer_p).wait_send()

    @pl.when(single)
    def _():
        coupled(1 - up, peer_p).wait_send()

    @pl.when(tells_last)
    def _():
        mirrored().wait_send()

    @pl.when(has_q)
    def _():
        head(1, slot_q, peer_q).wait_send()
        tail(1, slot_q, peer_q).wait_send()
        thin(1, slot_q, peer_q).wait_send()

    hand_down(lambda c: c.wait_send())
    for i, s in enumerate(bends):

        @pl.when(lax.rem(me + 2, 4 * s) == 0)
        def _():
            for part in range(PIECES):
                from_bend(i, part, me + 1 - 2 * s).wait_send()

    @pl.when(me > 0)
    def _():
        first_head(me - 1).wait_send()
        first_tail(me - 1).wait_send()
        first_thin(me - 1).wait_send()


def bend_strides(runs, total):
    stride = runs // 2
    return [stride] if stride > 1 and 4 * stride <= total else []


def local(runs, total, diag_blocks, coupling, rhs):
    slabs, order = diag_blocks.shape[1:3]
    half = order // 2
    columns = rhs.shape[3]
    depth = total.bit_length() - 1
    square, thin = (order, order), (order, columns)
    vmem = lambda *shape: pltpu.VMEM(shape, jnp.float32)
    dma = lambda n: pltpu.SemaphoreType.DMA((n,))
    slots = 1 + 2 * depth
    bends = len(bend_strides(runs, total))
    result = pl.pallas_call(
        functools.partial(kernel, runs, total),
        out_shape=jax.ShapeDtypeStruct(rhs.shape[1:], jnp.float32),
        in_specs=[pl.BlockSpec(memory_space=pltpu.VMEM)] * 3,
        out_specs=pl.BlockSpec(memory_space=pltpu.VMEM),
        scratch_shapes=[
            vmem(*square),
            vmem(*square),
            vmem(half, half),
            vmem(2, half, half),
            vmem(3, half, half),
            vmem(*thin),
            vmem(*square),
            vmem(*square),
            vmem(*square),
            vmem(slabs, *square),
            vmem(slabs, *square),
            vmem(slabs, *thin),
            vmem(2, 3, half, half),
            vmem(*square),
            vmem(*square),
            vmem(2, *thin),
            vmem(3, half, half),
            vmem(*thin),
            vmem(slots, 3, half, half),
            vmem(slots, *thin),
            vmem(2, *square),
            vmem(2, *thin),
            vmem(*thin),
            vmem(*thin),
            vmem(bends, *square),
            dma(8),
            dma(4),
            dma(slots),
            dma(bends * PIECES),
            dma(2 * slots),
            dma(slots),
            dma(2),
            dma(3),
            dma(bends * PIECES),
        ],
        compiler_params=pltpu.CompilerParams(collective_id=0, has_side_effects=True),
        name="chain_solve",
    )(diag_blocks[0], coupling[0], rhs[0])
    return result[None]


def solution(mesh):
    spec = P("seg", "run", None, None)
    runs = mesh.shape["run"]
    total = runs * mesh.shape["seg"]
    return jax.shard_map(
        functools.partial(local, runs, total),
        mesh=mesh,
        in_specs=(spec, spec, spec),
        out_specs=spec,
        check_vma=False,
    )
```

```python
import functools

import jax
import jax.numpy as jnp
from jax import lax
from jax.experimental import pallas as pl
from jax.experimental.pallas import tpu as pltpu
from jax.sharding import PartitionSpec as P

MESH = pl.DeviceIdType.MESH
HIGH = lax.Precision.HIGHEST
ROWS = 8
GROUPS = 2
PIECES = 4
PAUSE = 12
LANES = 128


def dot(a, b):
    return jnp.dot(a, b, precision=HIGH, preferred_element_type=jnp.float32)


def dot_nt(a, b):
    return lax.dot_general(
        a, b, (((1,), (1,)), ((), ())), precision=HIGH, preferred_element_type=jnp.float32
    )


def spread(x, shape):
    return jnp.broadcast_to(x, shape)


def total_of(terms):
    while len(terms) > 1:
        pairs = [terms[t] + terms[t + 1] for t in range(0, len(terms) - 1, 2)]
        terms = pairs + terms[len(pairs) * 2 :]
    return terms[0]


def three_parts(x):
    high = x.astype(jnp.bfloat16)
    rest = x - high.astype(jnp.float32)
    mid = rest.astype(jnp.bfloat16)
    low = (rest - mid.astype(jnp.float32)).astype(jnp.bfloat16)
    return [part.astype(jnp.float32) for part in (high, mid, low)]


def outer_product(left, right):
    lefts = list(zip(*[three_parts(x) for x in left]))
    rights = list(zip(*[three_parts(x) for x in right]))
    order = ((0, 0), (0, 1), (1, 0), (1, 1), (0, 2), (2, 0))
    stack = lambda parts, side: jnp.concatenate(
        [x for pair in order for x in parts[pair[side]]], axis=0
    ).astype(jnp.bfloat16)
    return lax.dot_general(
        stack(lefts, 0),
        stack(rights, 1),
        (((0,), (0,)), ((), ())),
        preferred_element_type=jnp.float32,
    )


def eliminate_panel(panel, first, sub, lane):
    shape = panel[0].shape
    groups = len(panel)
    width = groups * ROWS
    cols = [[spread(p[:, first + j : first + j + 1], shape) for p in panel] for j in range(width)]
    for col in cols:
        col[0] = jnp.where(lane >= 0, col[0], 0.0)
    inverses = [jnp.zeros(shape, jnp.float32)] * groups
    for j in range(width):
        own, row = divmod(j, ROWS)
        here = sub == row
        inverse = 1.0 / spread(cols[j][own][row : row + 1, :], shape)
        inverses[own] = jnp.where(here, inverse, inverses[own])
        factor = [jnp.where(here, 0.0, c) if i == own else c for i, c in enumerate(cols[j])]
        scaled = [f * inverse for f in factor]
        for m in range(j + 1, width):
            line = spread(cols[m][own][row : row + 1, :], shape)
            if m == j + 1:
                steps = [(f * line) * inverse for f in factor]
            else:
                steps = [f * line for f in scaled]
            cols[m] = [c - step for c, step in zip(cols[m], steps)]
        at = lane == first + j
        line = jnp.where(at, 1.0, spread(panel[own][row : row + 1, :], shape))
        unit = jnp.where(here, 1.0, 0.0)
        panel = [
            jnp.where(at, unit if i == own else 0.0, p) - scaled[i] * line
            for i, p in enumerate(panel)
        ]
    return [p * scale for p, scale in zip(panel, inverses)]


def spd_inverse_tile(rows):
    shape = rows[0].shape
    sub = lax.broadcasted_iota(jnp.int32, shape, 0)
    lane = lax.broadcasted_iota(jnp.int32, shape, 1)
    rows = list(rows)
    width = GROUPS * ROWS
    for k in range(0, len(rows), GROUPS):
        first = k * ROWS
        inside = jnp.logical_and(lane >= first, lane < first + width)
        panel = rows[k : k + GROUPS]
        columns = [
            jnp.where(lane < first, -p, jnp.where(inside, 0.0, p)) for p in panel
        ]
        panel = eliminate_panel(panel, first, sub, lane)
        near = range(k + GROUPS, min(k + 2 * GROUPS, len(rows)))
        for i in near:
            terms = [
                spread(rows[i][:, first + j : first + j + 1], shape)
                * spread(panel[j // ROWS][j % ROWS : j % ROWS + 1, :], shape)
                for j in range(width)
            ]
            rows[i] = jnp.where(inside, 0.0, rows[i]) - total_of(terms)
        update = outer_product(columns, panel)
        for i in range(len(rows)):
            if i < k or i >= k + 2 * GROUPS:
                rows[i] = jnp.where(inside, 0.0, rows[i]) - update[i * ROWS : (i + 1) * ROWS, :]
        rows[k : k + GROUPS] = panel
    return rows


def invert(node, x, tile, work, late):
    half = tile.shape[0]
    top, low = slice(0, half), slice(half, 2 * half)
    tile[...] = node[0]

    @pl.loop(0, 2)
    def _(step):
        rows = spd_inverse_tile([tile[i : i + ROWS, :] for i in range(0, half, ROWS)])
        for i, row in enumerate(rows):
            tile[i * ROWS : (i + 1) * ROWS, :] = row

        @pl.when(step == 0)
        def _():
            late()
            x[top, top] = tile[...]
            work[0] = dot(tile[...], node[1])
            work[1] = work[0].T
            tile[...] = node[2] - dot(work[1], node[1])

        @pl.when(step == 1)
        def _():
            corner = -dot(tile[...], work[1])
            x[low, low] = tile[...]
            x[low, top] = corner
            x[top, low] = -dot(work[0], tile[...])
            x[top, top] = x[top, top] - dot(work[0], corner)


def kernel(
    runs,
    total,
    diag,
    coup,
    rhs,
    out,
    first_x,
    x,
    tile,
    work,
    node,
    source,
    e_turned,
    w_p,
    w_q,
    keep_p,
    keep_q,
    keep_y,
    send_d,
    send_m,
    send_t,
    send_b,
    first_d,
    first_b,
    got_d,
    got_b,
    got_link,
    got_x,
    before,
    value,
    passing,
    far_k,
    far_y,
    sent,
    sent_first,
    sent_value,
    sent_pass,
    sent_far,
    come_d,
    come_b,
    come_m,
    come_x,
    come_pass,
    come_far,
):
    slabs, order = diag.shape[:2]
    inner = slabs - 1
    half = order // 2
    top, low = slice(0, half), slice(half, order)
    me = lax.axis_index("seg") * runs + lax.axis_index("run")
    depth = total.bit_length() - 1
    strides = [1 << i for i in range(depth)]
    last = me == total - 1
    inside = jnp.logical_not(last)
    pair = lax.rem(me + 1, total // 2) == 0
    single = jnp.logical_not(pair)
    tells_last = me == total - 1 - total // 4
    reach = total // 8
    gives = lax.rem(me + 1, 4 * reach) == 2 * reach
    takes = lax.rem(me + 1, 2 * reach) == reach
    even = lax.rem(me, 2) == 0
    odd = jnp.logical_not(even)
    steps = strides[:-1]
    parents = [lax.rem(me + 1, 2 * s) == 0 for s in steps]
    level = sum(jnp.where(parent, 1, 0) for parent in parents)
    span = 1 + sum(jnp.where(parent, s, 0) for s, parent in zip(steps, parents))
    next_above = lax.rem(me + span, 4 * span) == 2 * span - 1
    up = jnp.where(next_above, 1, 0)
    peer_p = jnp.where(next_above, me + span, me - span)
    peer_q = jnp.where(next_above, me - span, me + span)
    has_q = jnp.logical_and(peer_q >= 0, peer_q < total)
    slot_p = 1 + 2 * level + (1 - up)
    slot_q = 1 + 2 * level + up
    far = jnp.where(next_above, me + 3 * reach, me - 3 * reach)
    has_far = jnp.logical_and(far >= 0, far < total)
    bends = bend_strides(runs, total)
    piece = order // PIECES

    def copy(source_ref, target_ref, send_sem, recv_sem, peer):
        return pltpu.make_async_remote_copy(
            src_ref=source_ref,
            dst_ref=target_ref,
            send_sem=send_sem,
            recv_sem=recv_sem,
            device_id=(lax.rem(peer, runs), lax.div(peer, runs)),
            device_id_type=MESH,
        )

    barrier = pltpu.get_barrier_semaphore()
    met = [lax.rem(me + 1, s) == 0 for s in strides]
    greeted = [
        (jnp.logical_and(here, ok), peer)
        for s, here in zip(strides, met)
        for ok, peer in ((me >= s, me - s), (me + s < total, me + s))
    ]
    for peer in (me - 3 * reach, me + 3 * reach):
        ok = jnp.logical_and(peer >= 0, peer < total)
        greeted.append((jnp.logical_and(lax.rem(me + 1, 4 * reach) == 0, ok), peer))
    greeted.append((jnp.logical_and(takes, has_far), far))
    for s in bends:
        greeted.append((lax.rem(me + 1, 4 * s) == 3 * s, me + s - 1))
        greeted.append((lax.rem(me + 2, 4 * s) == 0, me + 1 - s))
        greeted.append((lax.rem(me + 2, 4 * s) == 0, me + 1 - 2 * s))
        greeted.append((lax.rem(me + 1, 4 * s) == 2 * s, me + 2 * s - 1))
    peers = sum(jnp.where(ok, 1, 0) for ok, _ in greeted)
    for ok, peer in greeted:

        @pl.when(ok)
        def _():
            pl.semaphore_signal(
                barrier,
                inc=1,
                device_id=(lax.rem(peer, runs), lax.div(peer, runs)),
                device_id_type=MESH,
            )

    def first_head(peer):
        return copy(first_d.at[0], got_d.at[0, 0], sent_first.at[0], come_d.at[0], peer)

    def first_tail(peer):
        return copy(
            first_d.at[pl.ds(1, 2)], got_d.at[0, pl.ds(1, 2)], sent_first.at[1], come_d.at[1], peer
        )

    def first_link(peer):
        return copy(send_m, got_link.at[1], sent_first.at[2], come_m.at[1], peer)

    def first_thin(peer):
        return copy(first_b, got_b.at[0], sent_first.at[3], come_b.at[0], peer)

    def head(role, slot, peer):
        return copy(
            send_d.at[role, 0], got_d.at[slot, 0], sent.at[role], come_d.at[2 * slot], peer
        )

    def tail(role, slot, peer):
        return copy(
            send_d.at[role, pl.ds(1, 2)],
            got_d.at[slot, pl.ds(1, 2)],
            sent.at[2 + role],
            come_d.at[2 * slot + 1],
            peer,
        )

    def thin(role, slot, peer):
        return copy(send_b.at[role], got_b.at[slot], sent.at[4 + role], come_b.at[slot], peer)

    def coupled(side, peer):
        return copy(send_m, got_link.at[side], sent.at[6], come_m.at[side], peer)

    def mirrored():
        return copy(send_t, got_link.at[0], sent.at[7], come_m.at[0], total - 1)

    def to_bend(which, part, peer):
        rows = pl.ds(part * piece, piece)
        return copy(
            send_m.at[rows],
            passing.at[which, rows],
            sent.at[6],
            come_pass.at[which * PIECES + part],
            peer,
        )

    def from_bend(which, part, peer):
        rows = pl.ds(part * piece, piece)
        return copy(
            passing.at[which, rows],
            got_link.at[1, rows],
            sent_pass.at[which * PIECES + part],
            come_m.at[1],
            peer,
        )

    def each_gift(act):
        for way, peer in enumerate((me - reach, me + reach)):
            for k, (source_ref, target_ref) in enumerate(
                (
                    (keep_p.at[inner], far_k.at[up]),
                    (keep_q.at[inner], far_k.at[1 - up]),
                    (keep_y.at[inner], far_y),
                )
            ):
                act(copy(source_ref, target_ref, sent_far.at[3 * way + k], come_far.at[k], peer))

    def each_source(act):
        @pl.when(inside)
        def _():
            act(0, me + 1)

        for i, s in enumerate(steps):
            for way, (ok, peer) in enumerate(((me >= s, me - s), (me + s < total, me + s))):

                @pl.when(jnp.logical_and(parents[i], ok))
                def _():
                    act(1 + 2 * i + way, peer)

    e_turned[...] = jnp.where(me == 0, jnp.zeros_like(coup[0]), coup[0]).T
    node[0] = diag[0, top, top]
    node[1] = diag[0, top, low]
    node[2] = diag[0, low, low]
    source[...] = rhs[0]
    for i in range(inner):
        final = i == inner - 1
        f_turned = coup.at[i + 1]
        invert(node, first_x, tile, work, lambda: None)
        w_p[...] = dot(e_turned[...], first_x[...])

        def put(block, rows, columns):
            term = dot_nt(w_p[rows, :], e_turned[columns, :])
            first_d[block] = -term if i == 0 else first_d[block] - term

        put(0, top, top)
        if final:
            pl.semaphore_wait(barrier, peers)

            @pl.when(me > 0)
            def _():
                first_head(me - 1).start()

        put(1, top, low)
        put(2, low, low)
        if final:

            @pl.when(me > 0)
            def _():
                first_tail(me - 1).start()

        w_q[...] = dot(f_turned[...], first_x[...])
        node[0] = diag[i + 1, top, top] - dot_nt(w_q[top, :], f_turned[top, :])
        node[1] = diag[i + 1, top, low] - dot_nt(w_q[top, :], f_turned[low, :])
        node[2] = diag[i + 1, low, low] - dot_nt(w_q[low, :], f_turned[low, :])

        def rest(i):
            f_turned = coup.at[i + 1]
            keep_y[i] = dot(first_x[...], source[...])
            term = dot(e_turned[...], keep_y[i])
            first_b[...] = -term if i == 0 else first_b[...] - term
            if i == inner - 1:

                @pl.when(me > 0)
                def _():
                    first_thin(me - 1).start()

            source[...] = rhs[i + 1] - dot(f_turned[...], keep_y[i])
            keep_p[i] = dot_nt(first_x[...], e_turned[...])
            keep_q[i] = dot_nt(first_x[...], f_turned[...])

        if final:

            @pl.when(odd)
            def _():
                send_m[...] = -dot_nt(w_q[...], e_turned[...])
                first_link(me - 1).start()
                rest(inner - 1)

            @pl.when(even)
            def _():
                got_link[0] = -dot_nt(w_p[...], f_turned[...])

        else:
            rest(i)
            e_turned[...] = -dot_nt(w_p[...], f_turned[...])

    def add_head(slot, peer):
        head(0, slot, peer).wait_recv()
        node[0] = node[0] + got_d[slot, 0]

    def add_tail(slot, peer):
        tail(0, slot, peer).wait_recv()
        node[1] = node[1] + got_d[slot, 1]
        node[2] = node[2] + got_d[slot, 2]

    def add_thin(slot, peer):
        thin(0, slot, peer).wait_recv()
        source[...] = source[...] + got_b[slot]

    each_source(add_head)
    invert(node, x, tile, work, lambda: each_source(add_tail))

    def serve_head(role, slot, peer, weights, turned):
        weights[top, :] = dot(turned[top, :], x[...])
        send_d[role, 0] = -dot_nt(weights[top, :], turned[top, :])
        head(role, slot, peer).start()

    def serve_tail(role, slot, peer, weights, turned):
        send_d[role, 1] = -dot_nt(weights[top, :], turned[low, :])
        weights[low, :] = dot(turned[low, :], x[...])
        send_d[role, 2] = -dot_nt(weights[low, :], turned[low, :])
        tail(role, slot, peer).start()

    @pl.when(inside)
    def _():
        coupled(1, me + 1).wait_recv()

    @pl.when(odd)
    def _():
        coupled(0, me - 1).wait_recv()
        first_link(me - 1).wait_send()

    to_p = (0, slot_p, peer_p, w_p, got_link.at[up])
    to_q = (1, slot_q, peer_q, w_q, got_link.at[1 - up])
    serve_head(*to_p)

    @pl.when(tells_last)
    def _():
        serve_head(*to_q)

    serve_tail(*to_p)

    @pl.when(tells_last)
    def _():
        serve_tail(*to_q)

    @pl.when(single)
    def _():
        send_m[...] = -dot_nt(got_link[1 - up], w_p[...])
        bent = [lax.rem(me + 1, 4 * s) == 3 * s for s in bends]
        for i, s in enumerate(bends):

            @pl.when(bent[i])
            def _():
                for part in range(PIECES):
                    to_bend(i, part, me + s - 1).start()

        straight = sum(jnp.where(b, 1, 0) for b in bent) == 0

        @pl.when(straight)
        def _():
            coupled(1 - up, peer_p).start()

        @pl.when(tells_last)
        def _():
            send_t[...] = -dot_nt(w_p[...], got_link[1 - up])
            mirrored().start()

        keep_p[inner] = dot_nt(x[...], got_link[up])
        keep_q[inner] = dot_nt(x[...], got_link[1 - up])

    @pl.when(even)
    def _():
        rest(inner - 1)

    each_source(add_thin)
    keep_y[inner] = dot(x[...], source[...])
    send_b[0] = -dot(got_link[up], keep_y[inner])
    thin(0, slot_p, peer_p).start()

    @pl.when(has_q)
    def _():

        @pl.when(jnp.logical_not(tells_last))
        def _():
            @pl.loop(0, jnp.where(level == 1, PAUSE, 0))
            def _(_):
                tile[...] = tile[...].T

            serve_head(*to_q)
            serve_tail(*to_q)

        send_b[1] = -dot(got_link[1 - up], keep_y[inner])
        thin(1, slot_q, peer_q).start()

    for i, s in enumerate(bends):

        @pl.when(lax.rem(me + 2, 4 * s) == 0)
        def _():
            for part in range(PIECES):
                to_bend(i, part, me).wait_recv()
                from_bend(i, part, me + 1 - 2 * s).start()

    @pl.when(gives)
    def _():
        each_gift(lambda c: c.start())

    @pl.when(single)
    def _():
        value[...] = keep_y[inner]

    @pl.when(takes)
    def _():
        for k, target_ref in enumerate((far_k.at[up], far_k.at[1 - up], far_y)):
            copy(target_ref, target_ref, sent_far.at[k], come_far.at[k], peer_p).wait_recv()
        value[...] = value[...] - dot(keep_p[inner], far_y[...])
        keep_q[inner] = keep_q[inner] - dot(keep_p[inner], far_k[1 - up])
        keep_p[inner] = -dot(keep_p[inner], far_k[up])

    @pl.when(single)
    def _():
        @pl.when(has_q)
        def _():
            copy(value, got_x.at[1], sent_value.at[0], come_x.at[1], peer_q).wait_recv()
            value[...] = value[...] - dot(keep_q[inner], got_x[1])

        @pl.when(jnp.logical_or(jnp.logical_not(takes), has_far))
        def _():
            copy(value, got_x.at[0], sent_value.at[0], come_x.at[0], peer_p).wait_recv()
            value[...] = value[...] - dot(keep_p[inner], got_x[0])

    @pl.when(pair)
    def _():
        slot = 1 + 2 * level + up
        add_head(slot, peer_p)
        invert(node, x, tile, work, lambda: add_tail(slot, peer_p))
        add_thin(slot, peer_p)
        value[...] = dot(x[...], source[...])

    def hand_down(act):
        def near(i, s):
            role = jnp.where(jnp.logical_and(level == i + 1, inside), 0, 1)
            tells = parents[i]
            if s == reach:
                tells = jnp.logical_and(tells, jnp.logical_not(gives))
            for way, (ok, peer) in enumerate(((me >= s, me - s), (me + s < total, me + s))):

                @pl.when(jnp.logical_and(tells, ok))
                def _():
                    act(
                        copy(
                            value, got_x.at[role], sent_value.at[2 * i + way], come_x.at[role], peer
                        )
                    )

        order_of = list(enumerate(steps))
        near(*order_of[-2])
        for way, peer in enumerate((me - 3 * reach, me + 3 * reach)):
            ok = jnp.logical_and(peer >= 0, peer < total)

            @pl.when(jnp.logical_and(lax.rem(me + 1, 4 * reach) == 0, ok))
            def _():
                act(copy(value, got_x.at[0], sent_far.at[6 + way], come_x.at[0], peer))

        near(*order_of[-1])
        for i, s in reversed(order_of[:-2]):
            near(i, s)

        @pl.when(even)
        def _():
            act(copy(value, before, sent_value.at[2 * depth], come_x.at[2], me + 1))

    hand_down(lambda c: c.start())
    out[inner] = value[...]
    for i in reversed(range(inner)):
        out[i] = keep_y[i] - dot(keep_q[i], out[i + 1])

    @pl.when(jnp.logical_and(even, me > 0))
    def _():
        for i in reversed(range(inner)):
            out[i] = out[i] - dot(keep_p[i], got_x[up])

    @pl.when(odd)
    def _():
        copy(value, before, sent_value.at[2 * depth], come_x.at[2], me - 1).wait_recv()
        for i in reversed(range(inner)):
            out[i] = out[i] - dot(keep_p[i], before[...])

    head(0, slot_p, peer_p).wait_send()
    tail(0, slot_p, peer_p).wait_send()
    thin(0, slot_p, peer_p).wait_send()

    @pl.when(single)
    def _():
        coupled(1 - up, peer_p).wait_send()

    @pl.when(tells_last)
    def _():
        mirrored().wait_send()

    @pl.when(gives)
    def _():
        each_gift(lambda c: c.wait_send())

    @pl.when(has_q)
    def _():
        head(1, slot_q, peer_q).wait_send()
        tail(1, slot_q, peer_q).wait_send()
        thin(1, slot_q, peer_q).wait_send()

    hand_down(lambda c: c.wait_send())
    for i, s in enumerate(bends):

        @pl.when(lax.rem(me + 2, 4 * s) == 0)
        def _():
            for part in range(PIECES):
                from_bend(i, part, me + 1 - 2 * s).wait_send()

    @pl.when(me > 0)
    def _():
        first_head(me - 1).wait_send()
        first_tail(me - 1).wait_send()
        first_thin(me - 1).wait_send()


def bend_strides(runs, total):
    stride = runs // 2
    return [stride] if stride > 1 and 4 * stride <= total else []


def local(runs, total, diag_blocks, coupling, rhs):
    slabs, order = diag_blocks.shape[1:3]
    half = order // 2
    columns = rhs.shape[3]
    depth = total.bit_length() - 1
    square, thin = (order, order), (order, columns)
    vmem = lambda *shape: pltpu.VMEM(shape, jnp.float32)
    dma = lambda n: pltpu.SemaphoreType.DMA((n,))
    slots = 1 + 2 * depth
    bends = len(bend_strides(runs, total))
    result = pl.pallas_call(
        functools.partial(kernel, runs, total),
        out_shape=jax.ShapeDtypeStruct(rhs.shape[1:], jnp.float32),
        in_specs=[pl.BlockSpec(memory_space=pltpu.VMEM)] * 3,
        out_specs=pl.BlockSpec(memory_space=pltpu.VMEM),
        scratch_shapes=[
            vmem(*square),
            vmem(*square),
            vmem(half, half),
            vmem(2, half, half),
            vmem(3, half, half),
            vmem(*thin),
            vmem(*square),
            vmem(*square),
            vmem(*square),
            vmem(slabs, *square),
            vmem(slabs, *square),
            vmem(slabs, *thin),
            vmem(2, 3, half, half),
            vmem(*square),
            vmem(*square),
            vmem(2, *thin),
            vmem(3, half, half),
            vmem(*thin),
            vmem(slots, 3, half, half),
            vmem(slots, *thin),
            vmem(2, *square),
            vmem(2, *thin),
            vmem(*thin),
            vmem(*thin),
            vmem(bends, *square),
            vmem(2, *square),
            vmem(*thin),
            dma(8),
            dma(4),
            dma(slots),
            dma(bends * PIECES),
            dma(8),
            dma(2 * slots),
            dma(slots),
            dma(2),
            dma(3),
            dma(bends * PIECES),
            dma(3),
        ],
        compiler_params=pltpu.CompilerParams(collective_id=0, has_side_effects=True),
        name="chain_solve",
    )(diag_blocks[0], coupling[0], rhs[0])
    return result[None]


def solution(mesh):
    spec = P("seg", "run", None, None)
    runs = mesh.shape["run"]
    total = runs * mesh.shape["seg"]
    return jax.shard_map(
        functools.partial(local, runs, total),
        mesh=mesh,
        in_specs=(spec, spec, spec),
        out_specs=spec,
        check_vma=False,
    )
```

```python
import functools

import jax
import jax.numpy as jnp
from jax import lax
from jax.experimental import pallas as pl
from jax.experimental.pallas import tpu as pltpu
from jax.sharding import PartitionSpec as P

MESH = pl.DeviceIdType.MESH
HIGH = lax.Precision.HIGHEST
ROWS = 8
GROUPS = 2
PIECES = 4
PAUSE = 8
LANES = 128


def dot(a, b):
    return jnp.dot(a, b, precision=HIGH, preferred_element_type=jnp.float32)


def dot_nt(a, b):
    return lax.dot_general(
        a, b, (((1,), (1,)), ((), ())), precision=HIGH, preferred_element_type=jnp.float32
    )


def spread(x, shape):
    return jnp.broadcast_to(x, shape)


def total_of(terms):
    while len(terms) > 1:
        pairs = [terms[t] + terms[t + 1] for t in range(0, len(terms) - 1, 2)]
        terms = pairs + terms[len(pairs) * 2 :]
    return terms[0]


def three_parts(x):
    high = x.astype(jnp.bfloat16)
    rest = x - high.astype(jnp.float32)
    mid = rest.astype(jnp.bfloat16)
    low = (rest - mid.astype(jnp.float32)).astype(jnp.bfloat16)
    return [part.astype(jnp.float32) for part in (high, mid, low)]


def outer_product(left, right):
    lefts = list(zip(*[three_parts(x) for x in left]))
    rights = list(zip(*[three_parts(x) for x in right]))
    order = ((0, 0), (0, 1), (1, 0), (1, 1), (0, 2), (2, 0))
    stack = lambda parts, side: jnp.concatenate(
        [x for pair in order for x in parts[pair[side]]], axis=0
    ).astype(jnp.bfloat16)
    return lax.dot_general(
        stack(lefts, 0),
        stack(rights, 1),
        (((0,), (0,)), ((), ())),
        preferred_element_type=jnp.float32,
    )


def eliminate_panel(panel, first, sub, lane):
    shape = panel[0].shape
    groups = len(panel)
    width = groups * ROWS
    cols = [[spread(p[:, first + j : first + j + 1], shape) for p in panel] for j in range(width)]
    cols[0] = [jnp.where(lane >= 0, c, 0.0) for c in cols[0]]
    inverses = [jnp.zeros(shape, jnp.float32)] * groups
    for j in range(width):
        own, row = divmod(j, ROWS)
        here = sub == row
        inverse = 1.0 / spread(cols[j][own][row : row + 1, :], shape)
        inverses[own] = jnp.where(here, inverse, inverses[own])
        factor = [jnp.where(here, 0.0, c) if i == own else c for i, c in enumerate(cols[j])]
        scaled = [f * inverse for f in factor]
        for m in range(j + 1, width):
            at_m, row_m = divmod(m, ROWS)
            line = spread(cols[j][at_m][row_m : row_m + 1, :], shape)
            if m == j + 1:
                steps = [(f * line) * inverse for f in factor]
            else:
                steps = [f * line for f in scaled]
            cols[m] = [c - step for c, step in zip(cols[m], steps)]
        at = lane == first + j
        line = jnp.where(at, 1.0, spread(panel[own][row : row + 1, :], shape))
        unit = jnp.where(here, 1.0, 0.0)
        panel = [
            jnp.where(at, unit if i == own else 0.0, p) - scaled[i] * line
            for i, p in enumerate(panel)
        ]
    return [p * scale for p, scale in zip(panel, inverses)]


def spd_inverse_tile(rows):
    shape = rows[0].shape
    sub = lax.broadcasted_iota(jnp.int32, shape, 0)
    lane = lax.broadcasted_iota(jnp.int32, shape, 1)
    rows = list(rows)
    width = GROUPS * ROWS
    for k in range(0, len(rows), GROUPS):
        first = k * ROWS
        inside = jnp.logical_and(lane >= first, lane < first + width)
        panel = rows[k : k + GROUPS]
        columns = [
            jnp.where(lane < first, -p, jnp.where(inside, 0.0, p)) for p in panel
        ]
        panel = eliminate_panel(panel, first, sub, lane)
        near = range(k + GROUPS, min(k + 2 * GROUPS, len(rows)))
        for i in near:
            terms = [
                spread(rows[i][:, first + j : first + j + 1], shape)
                * spread(panel[j // ROWS][j % ROWS : j % ROWS + 1, :], shape)
                for j in range(width)
            ]
            rows[i] = jnp.where(inside, 0.0, rows[i]) - total_of(terms)
        update = outer_product(columns, panel)
        for i in range(len(rows)):
            if i < k or i >= k + 2 * GROUPS:
                rows[i] = jnp.where(inside, 0.0, rows[i]) - update[i * ROWS : (i + 1) * ROWS, :]
        rows[k : k + GROUPS] = panel
    return rows


def invert(node, x, tile, work, late):
    half = tile.shape[0]
    top, low = slice(0, half), slice(half, 2 * half)
    tile[...] = node[0]

    @pl.loop(0, 2)
    def _(step):
        rows = spd_inverse_tile([tile[i : i + ROWS, :] for i in range(0, half, ROWS)])
        for i, row in enumerate(rows):
            tile[i * ROWS : (i + 1) * ROWS, :] = row

        @pl.when(step == 0)
        def _():
            late()
            x[top, top] = tile[...]
            work[0] = dot(tile[...], node[1])
            work[1] = work[0].T
            tile[...] = node[2] - dot(work[1], node[1])

        @pl.when(step == 1)
        def _():
            corner = -dot(tile[...], work[1])
            x[low, low] = tile[...]
            x[low, top] = corner
            x[top, low] = -dot(work[0], tile[...])
            x[top, top] = x[top, top] - dot(work[0], corner)


def kernel(
    runs,
    total,
    diag,
    coup,
    rhs,
    out,
    first_x,
    x,
    tile,
    work,
    node,
    source,
    e_turned,
    w_p,
    w_q,
    keep_p,
    keep_q,
    keep_y,
    send_d,
    send_m,
    send_t,
    send_b,
    first_d,
    first_b,
    got_d,
    got_b,
    got_link,
    got_x,
    before,
    value,
    passing,
    far_k,
    far_y,
    sent,
    sent_first,
    sent_value,
    sent_pass,
    sent_far,
    come_d,
    come_b,
    come_m,
    come_x,
    come_pass,
    come_far,
):
    slabs, order = diag.shape[:2]
    inner = slabs - 1
    half = order // 2
    top, low = slice(0, half), slice(half, order)
    me = lax.axis_index("seg") * runs + lax.axis_index("run")
    depth = total.bit_length() - 1
    strides = [1 << i for i in range(depth)]
    last = me == total - 1
    inside = jnp.logical_not(last)
    pair = lax.rem(me + 1, total // 2) == 0
    single = jnp.logical_not(pair)
    tells_last = me == total - 1 - total // 4
    reach = total // 8
    gives = lax.rem(me + 1, 4 * reach) == 2 * reach
    takes = lax.rem(me + 1, 2 * reach) == reach
    even = lax.rem(me, 2) == 0
    odd = jnp.logical_not(even)
    steps = strides[:-1]
    parents = [lax.rem(me + 1, 2 * s) == 0 for s in steps]
    level = sum(jnp.where(parent, 1, 0) for parent in parents)
    span = 1 + sum(jnp.where(parent, s, 0) for s, parent in zip(steps, parents))
    next_above = lax.rem(me + span, 4 * span) == 2 * span - 1
    up = jnp.where(next_above, 1, 0)
    peer_p = jnp.where(next_above, me + span, me - span)
    peer_q = jnp.where(next_above, me - span, me + span)
    has_q = jnp.logical_and(peer_q >= 0, peer_q < total)
    slot_p = 1 + 2 * level + (1 - up)
    slot_q = 1 + 2 * level + up
    far = jnp.where(next_above, me + 3 * reach, me - 3 * reach)
    has_far = jnp.logical_and(far >= 0, far < total)
    bends = bend_strides(runs, total)
    piece = order // PIECES

    def copy(source_ref, target_ref, send_sem, recv_sem, peer):
        return pltpu.make_async_remote_copy(
            src_ref=source_ref,
            dst_ref=target_ref,
            send_sem=send_sem,
            recv_sem=recv_sem,
            device_id=(lax.rem(peer, runs), lax.div(peer, runs)),
            device_id_type=MESH,
        )

    barrier = pltpu.get_barrier_semaphore()
    met = [lax.rem(me + 1, s) == 0 for s in strides]
    greeted = [
        (jnp.logical_and(here, ok), peer)
        for s, here in zip(strides, met)
        for ok, peer in ((me >= s, me - s), (me + s < total, me + s))
    ]
    for peer in (me - 3 * reach, me + 3 * reach):
        ok = jnp.logical_and(peer >= 0, peer < total)
        greeted.append((jnp.logical_and(lax.rem(me + 1, 4 * reach) == 0, ok), peer))
    greeted.append((jnp.logical_and(takes, has_far), far))
    for s in bends:
        greeted.append((lax.rem(me + 1, 4 * s) == 3 * s, me + s - 1))
        greeted.append((lax.rem(me + 2, 4 * s) == 0, me + 1 - s))
        greeted.append((lax.rem(me + 2, 4 * s) == 0, me + 1 - 2 * s))
        greeted.append((lax.rem(me + 1, 4 * s) == 2 * s, me + 2 * s - 1))
    peers = sum(jnp.where(ok, 1, 0) for ok, _ in greeted)
    for ok, peer in greeted:

        @pl.when(ok)
        def _():
            pl.semaphore_signal(
                barrier,
                inc=1,
                device_id=(lax.rem(peer, runs), lax.div(peer, runs)),
                device_id_type=MESH,
            )

    def first_head(peer):
        return copy(first_d.at[0], got_d.at[0, 0], sent_first.at[0], come_d.at[0], peer)

    def first_tail(peer):
        return copy(
            first_d.at[pl.ds(1, 2)], got_d.at[0, pl.ds(1, 2)], sent_first.at[1], come_d.at[1], peer
        )

    def first_link(peer):
        return copy(send_m, got_link.at[1], sent_first.at[2], come_m.at[1], peer)

    def first_thin(peer):
        return copy(first_b, got_b.at[0], sent_first.at[3], come_b.at[0], peer)

    def head(role, slot, peer):
        return copy(
            send_d.at[role, 0], got_d.at[slot, 0], sent.at[role], come_d.at[2 * slot], peer
        )

    def tail(role, slot, peer):
        return copy(
            send_d.at[role, pl.ds(1, 2)],
            got_d.at[slot, pl.ds(1, 2)],
            sent.at[2 + role],
            come_d.at[2 * slot + 1],
            peer,
        )

    def thin(role, slot, peer):
        return copy(send_b.at[role], got_b.at[slot], sent.at[4 + role], come_b.at[slot], peer)

    def coupled(side, peer):
        return copy(send_m, got_link.at[side], sent.at[6], come_m.at[side], peer)

    def mirrored():
        return copy(send_t, got_link.at[0], sent.at[7], come_m.at[0], total - 1)

    def to_bend(which, part, peer):
        rows = pl.ds(part * piece, piece)
        return copy(
            send_m.at[rows],
            passing.at[which, rows],
            sent.at[6],
            come_pass.at[which * PIECES + part],
            peer,
        )

    def from_bend(which, part, peer):
        rows = pl.ds(part * piece, piece)
        return copy(
            passing.at[which, rows],
            got_link.at[1, rows],
            sent_pass.at[which * PIECES + part],
            come_m.at[1],
            peer,
        )

    def each_gift(act):
        for way, peer in enumerate((me - reach, me + reach)):
            for k, (source_ref, target_ref) in enumerate(
                (
                    (keep_p.at[inner], far_k.at[up]),
                    (keep_q.at[inner], far_k.at[1 - up]),
                    (keep_y.at[inner], far_y),
                )
            ):
                act(copy(source_ref, target_ref, sent_far.at[3 * way + k], come_far.at[k], peer))

    def each_source(act):
        @pl.when(inside)
        def _():
            act(0, me + 1)

        for i, s in enumerate(steps):
            for way, (ok, peer) in enumerate(((me >= s, me - s), (me + s < total, me + s))):

                @pl.when(jnp.logical_and(parents[i], ok))
                def _():
                    act(1 + 2 * i + way, peer)

    e_turned[...] = jnp.where(me == 0, jnp.zeros_like(coup[0]), coup[0]).T
    node[0] = diag[0, top, top]
    node[1] = diag[0, top, low]
    node[2] = diag[0, low, low]
    source[...] = rhs[0]
    for i in range(inner):
        final = i == inner - 1
        f_turned = coup.at[i + 1]
        invert(node, first_x, tile, work, lambda: None)
        w_p[...] = dot(e_turned[...], first_x[...])

        def put(block, rows, columns):
            term = dot_nt(w_p[rows, :], e_turned[columns, :])
            first_d[block] = -term if i == 0 else first_d[block] - term

        put(0, top, top)
        if final:
            pl.semaphore_wait(barrier, peers)

            @pl.when(me > 0)
            def _():
                first_head(me - 1).start()

        put(1, top, low)
        put(2, low, low)
        if final:

            @pl.when(me > 0)
            def _():
                first_tail(me - 1).start()

        w_q[...] = dot(f_turned[...], first_x[...])
        node[0] = diag[i + 1, top, top] - dot_nt(w_q[top, :], f_turned[top, :])
        node[1] = diag[i + 1, top, low] - dot_nt(w_q[top, :], f_turned[low, :])
        node[2] = diag[i + 1, low, low] - dot_nt(w_q[low, :], f_turned[low, :])

        def rest(i):
            f_turned = coup.at[i + 1]
            keep_y[i] = dot(first_x[...], source[...])
            term = dot(e_turned[...], keep_y[i])
            first_b[...] = -term if i == 0 else first_b[...] - term
            if i == inner - 1:

                @pl.when(me > 0)
                def _():
                    first_thin(me - 1).start()

            source[...] = rhs[i + 1] - dot(f_turned[...], keep_y[i])
            keep_p[i] = dot_nt(first_x[...], e_turned[...])
            keep_q[i] = dot_nt(first_x[...], f_turned[...])

        if final:

            @pl.when(odd)
            def _():
                send_m[...] = -dot_nt(w_q[...], e_turned[...])
                first_link(me - 1).start()
                rest(inner - 1)

            @pl.when(even)
            def _():
                got_link[0] = -dot_nt(w_p[...], f_turned[...])

        else:
            rest(i)
            e_turned[...] = -dot_nt(w_p[...], f_turned[...])

    def add_head(slot, peer):
        head(0, slot, peer).wait_recv()
        node[0] = node[0] + got_d[slot, 0]

    def add_tail(slot, peer):
        tail(0, slot, peer).wait_recv()
        node[1] = node[1] + got_d[slot, 1]
        node[2] = node[2] + got_d[slot, 2]

    def add_thin(slot, peer):
        thin(0, slot, peer).wait_recv()
        source[...] = source[...] + got_b[slot]

    each_source(add_head)
    invert(node, x, tile, work, lambda: each_source(add_tail))

    def serve_head(role, slot, peer, weights, turned):
        weights[top, :] = dot(turned[top, :], x[...])
        send_d[role, 0] = -dot_nt(weights[top, :], turned[top, :])
        head(role, slot, peer).start()

    def serve_tail(role, slot, peer, weights, turned):
        send_d[role, 1] = -dot_nt(weights[top, :], turned[low, :])
        weights[low, :] = dot(turned[low, :], x[...])
        send_d[role, 2] = -dot_nt(weights[low, :], turned[low, :])
        tail(role, slot, peer).start()

    @pl.when(inside)
    def _():
        coupled(1, me + 1).wait_recv()

    @pl.when(odd)
    def _():
        coupled(0, me - 1).wait_recv()
        first_link(me - 1).wait_send()

    to_p = (0, slot_p, peer_p, w_p, got_link.at[up])
    to_q = (1, slot_q, peer_q, w_q, got_link.at[1 - up])
    serve_head(*to_p)

    @pl.when(tells_last)
    def _():
        serve_head(*to_q)

    serve_tail(*to_p)

    @pl.when(tells_last)
    def _():
        serve_tail(*to_q)

    @pl.when(single)
    def _():
        send_m[...] = -dot_nt(got_link[1 - up], w_p[...])
        bent = [lax.rem(me + 1, 4 * s) == 3 * s for s in bends]
        for i, s in enumerate(bends):

            @pl.when(bent[i])
            def _():
                for part in range(PIECES):
                    to_bend(i, part, me + s - 1).start()

        straight = sum(jnp.where(b, 1, 0) for b in bent) == 0

        @pl.when(straight)
        def _():
            coupled(1 - up, peer_p).start()

        @pl.when(tells_last)
        def _():
            send_t[...] = -dot_nt(w_p[...], got_link[1 - up])
            mirrored().start()

        keep_p[inner] = dot_nt(x[...], got_link[up])
        keep_q[inner] = dot_nt(x[...], got_link[1 - up])

    @pl.when(even)
    def _():
        rest(inner - 1)

    each_source(add_thin)
    keep_y[inner] = dot(x[...], source[...])
    send_b[0] = -dot(got_link[up], keep_y[inner])
    thin(0, slot_p, peer_p).start()

    @pl.when(has_q)
    def _():

        @pl.when(jnp.logical_not(tells_last))
        def _():
            @pl.loop(0, jnp.where(level == 1, PAUSE, 0))
            def _(_):
                tile[...] = tile[...].T

            serve_head(*to_q)
            serve_tail(*to_q)

        send_b[1] = -dot(got_link[1 - up], keep_y[inner])
        thin(1, slot_q, peer_q).start()

    for i, s in enumerate(bends):

        @pl.when(lax.rem(me + 2, 4 * s) == 0)
        def _():
            for part in range(PIECES):
                to_bend(i, part, me).wait_recv()
                from_bend(i, part, me + 1 - 2 * s).start()

    @pl.when(gives)
    def _():
        each_gift(lambda c: c.start())

    @pl.when(single)
    def _():
        value[...] = keep_y[inner]

    @pl.when(takes)
    def _():
        for k, target_ref in enumerate((far_k.at[up], far_k.at[1 - up], far_y)):
            copy(target_ref, target_ref, sent_far.at[k], come_far.at[k], peer_p).wait_recv()
        value[...] = value[...] - dot(keep_p[inner], far_y[...])
        keep_q[inner] = keep_q[inner] - dot(keep_p[inner], far_k[1 - up])
        keep_p[inner] = -dot(keep_p[inner], far_k[up])

    passes = jnp.logical_and(level == 1, me >= 2)

    def passed(side):
        return copy(got_x.at[side], got_x.at[1], sent_pass.at[len(bends) * PIECES], come_x.at[1], me - 1)

    @pl.when(single)
    def _():
        @pl.when(has_q)
        def _():
            copy(value, got_x.at[1], sent_value.at[0], come_x.at[1], peer_q).wait_recv()

            @pl.when(jnp.logical_and(passes, up == 1))
            def _():
                passed(1).start()

            value[...] = value[...] - dot(keep_q[inner], got_x[1])

        @pl.when(jnp.logical_or(jnp.logical_not(takes), has_far))
        def _():
            copy(value, got_x.at[0], sent_value.at[0], come_x.at[0], peer_p).wait_recv()

            @pl.when(jnp.logical_and(passes, up == 0))
            def _():
                passed(0).start()

            value[...] = value[...] - dot(keep_p[inner], got_x[0])

    @pl.when(pair)
    def _():
        slot = 1 + 2 * level + up
        add_head(slot, peer_p)
        invert(node, x, tile, work, lambda: add_tail(slot, peer_p))
        add_thin(slot, peer_p)
        value[...] = dot(x[...], source[...])

    def hand_down(act):
        def near(i, s):
            role = jnp.where(jnp.logical_and(level == i + 1, inside), 0, 1)
            tells = parents[i]
            if s == reach:
                tells = jnp.logical_and(tells, jnp.logical_not(gives))
            for way, (ok, peer) in enumerate(((me >= s, me - s), (me + s < total, me + s))):
                if s == 1 and way == 1:
                    ok = jnp.logical_and(ok, level == 1)

                @pl.when(jnp.logical_and(tells, ok))
                def _():
                    act(
                        copy(
                            value, got_x.at[role], sent_value.at[2 * i + way], come_x.at[role], peer
                        )
                    )

        order_of = list(enumerate(steps))
        near(*order_of[-2])
        for way, peer in enumerate((me - 3 * reach, me + 3 * reach)):
            ok = jnp.logical_and(peer >= 0, peer < total)

            @pl.when(jnp.logical_and(lax.rem(me + 1, 4 * reach) == 0, ok))
            def _():
                act(copy(value, got_x.at[0], sent_far.at[6 + way], come_x.at[0], peer))

        near(*order_of[-1])
        for i, s in reversed(order_of[:-2]):
            near(i, s)

        @pl.when(even)
        def _():
            act(copy(value, before, sent_value.at[2 * depth], come_x.at[2], me + 1))

    hand_down(lambda c: c.start())
    out[inner] = value[...]
    for i in reversed(range(inner)):
        out[i] = keep_y[i] - dot(keep_q[i], out[i + 1])

    @pl.when(jnp.logical_and(even, me > 0))
    def _():
        for i in reversed(range(inner)):
            out[i] = out[i] - dot(keep_p[i], got_x[up])

    @pl.when(odd)
    def _():
        copy(value, before, sent_value.at[2 * depth], come_x.at[2], me - 1).wait_recv()
        for i in reversed(range(inner)):
            out[i] = out[i] - dot(keep_p[i], before[...])

    head(0, slot_p, peer_p).wait_send()
    tail(0, slot_p, peer_p).wait_send()
    thin(0, slot_p, peer_p).wait_send()

    @pl.when(single)
    def _():
        coupled(1 - up, peer_p).wait_send()

    @pl.when(tells_last)
    def _():
        mirrored().wait_send()

    @pl.when(gives)
    def _():
        each_gift(lambda c: c.wait_send())

    @pl.when(passes)
    def _():
        passed(0).wait_send()

    @pl.when(has_q)
    def _():
        head(1, slot_q, peer_q).wait_send()
        tail(1, slot_q, peer_q).wait_send()
        thin(1, slot_q, peer_q).wait_send()

    hand_down(lambda c: c.wait_send())
    for i, s in enumerate(bends):

        @pl.when(lax.rem(me + 2, 4 * s) == 0)
        def _():
            for part in range(PIECES):
                from_bend(i, part, me + 1 - 2 * s).wait_send()

    @pl.when(me > 0)
    def _():
        first_head(me - 1).wait_send()
        first_tail(me - 1).wait_send()
        first_thin(me - 1).wait_send()


def bend_strides(runs, total):
    stride = runs // 2
    return [stride] if stride > 1 and 4 * stride <= total else []


def local(runs, total, diag_blocks, coupling, rhs):
    slabs, order = diag_blocks.shape[1:3]
    half = order // 2
    columns = rhs.shape[3]
    depth = total.bit_length() - 1
    square, thin = (order, order), (order, columns)
    vmem = lambda *shape: pltpu.VMEM(shape, jnp.float32)
    dma = lambda n: pltpu.SemaphoreType.DMA((n,))
    slots = 1 + 2 * depth
    bends = len(bend_strides(runs, total))
    result = pl.pallas_call(
        functools.partial(kernel, runs, total),
        out_shape=jax.ShapeDtypeStruct(rhs.shape[1:], jnp.float32),
        in_specs=[pl.BlockSpec(memory_space=pltpu.VMEM)] * 3,
        out_specs=pl.BlockSpec(memory_space=pltpu.VMEM),
        scratch_shapes=[
            vmem(*square),
            vmem(*square),
            vmem(half, half),
            vmem(2, half, half),
            vmem(3, half, half),
            vmem(*thin),
            vmem(*square),
            vmem(*square),
            vmem(*square),
            vmem(slabs, *square),
            vmem(slabs, *square),
            vmem(slabs, *thin),
            vmem(2, 3, half, half),
            vmem(*square),
            vmem(*square),
            vmem(2, *thin),
            vmem(3, half, half),
            vmem(*thin),
            vmem(slots, 3, half, half),
            vmem(slots, *thin),
            vmem(2, *square),
            vmem(2, *thin),
            vmem(*thin),
            vmem(*thin),
            vmem(bends, *square),
            vmem(2, *square),
            vmem(*thin),
            dma(8),
            dma(4),
            dma(slots),
            dma(bends * PIECES + 1),
            dma(8),
            dma(2 * slots),
            dma(slots),
            dma(2),
            dma(3),
            dma(bends * PIECES),
            dma(3),
        ],
        compiler_params=pltpu.CompilerParams(collective_id=0, has_side_effects=True),
        name="chain_solve",
    )(diag_blocks[0], coupling[0], rhs[0])
    return result[None]


def solution(mesh):
    spec = P("seg", "run", None, None)
    runs = mesh.shape["run"]
    total = runs * mesh.shape["seg"]
    return jax.shard_map(
        functools.partial(local, runs, total),
        mesh=mesh,
        in_specs=(spec, spec, spec),
        out_specs=spec,
        check_vma=False,
    )
```

```python
import functools

import jax
import jax.numpy as jnp
from jax import lax
from jax.experimental import pallas as pl
from jax.experimental.pallas import tpu as pltpu
from jax.sharding import PartitionSpec as P

MESH = pl.DeviceIdType.MESH
HIGH = lax.Precision.HIGHEST
ROWS = 8
GROUPS = 2
PIECES = 4
PAUSE = 11
PAUSE_THIN = 20
LANES = 128


def dot(a, b):
    return jnp.dot(a, b, precision=HIGH, preferred_element_type=jnp.float32)


def dot_nt(a, b):
    return lax.dot_general(
        a, b, (((1,), (1,)), ((), ())), precision=HIGH, preferred_element_type=jnp.float32
    )


def spread(x, shape):
    return jnp.broadcast_to(x, shape)


def total_of(terms):
    while len(terms) > 1:
        pairs = [terms[t] + terms[t + 1] for t in range(0, len(terms) - 1, 2)]
        terms = pairs + terms[len(pairs) * 2 :]
    return terms[0]


def three_parts(x):
    high = x.astype(jnp.bfloat16)
    rest = x - high.astype(jnp.float32)
    mid = rest.astype(jnp.bfloat16)
    low = (rest - mid.astype(jnp.float32)).astype(jnp.bfloat16)
    return [part.astype(jnp.float32) for part in (high, mid, low)]


def outer_product(left, right):
    lefts = list(zip(*[three_parts(x) for x in left]))
    rights = list(zip(*[three_parts(x) for x in right]))
    order = ((0, 0), (0, 1), (1, 0), (1, 1), (0, 2), (2, 0))
    stack = lambda parts, side: jnp.concatenate(
        [x for pair in order for x in parts[pair[side]]], axis=0
    ).astype(jnp.bfloat16)
    return lax.dot_general(
        stack(lefts, 0),
        stack(rights, 1),
        (((0,), (0,)), ((), ())),
        preferred_element_type=jnp.float32,
    )


def eliminate_panel(panel, first, sub, lane):
    shape = panel[0].shape
    groups = len(panel)
    width = groups * ROWS
    cols = [[spread(p[:, first + j : first + j + 1], shape) for p in panel] for j in range(width)]
    cols[0] = [jnp.where(lane >= 0, c, 0.0) for c in cols[0]]
    inverses = [jnp.zeros(shape, jnp.float32)] * groups
    for j in range(width):
        own, row = divmod(j, ROWS)
        here = sub == row
        inverse = 1.0 / spread(cols[j][own][row : row + 1, :], shape)
        inverses[own] = jnp.where(here, inverse, inverses[own])
        factor = [jnp.where(here, 0.0, c) if i == own else c for i, c in enumerate(cols[j])]
        scaled = [f * inverse for f in factor]
        for m in range(j + 1, width):
            at_m, row_m = divmod(m, ROWS)
            line = spread(cols[j][at_m][row_m : row_m + 1, :], shape)
            if m == j + 1:
                steps = [(f * line) * inverse for f in factor]
            else:
                steps = [f * line for f in scaled]
            cols[m] = [c - step for c, step in zip(cols[m], steps)]
        at = lane == first + j
        line = jnp.where(at, 1.0, spread(panel[own][row : row + 1, :], shape))
        unit = jnp.where(here, 1.0, 0.0)
        panel = [
            jnp.where(at, unit if i == own else 0.0, p) - scaled[i] * line
            for i, p in enumerate(panel)
        ]
    return [p * scale for p, scale in zip(panel, inverses)]


def spd_inverse_tile(rows):
    shape = rows[0].shape
    sub = lax.broadcasted_iota(jnp.int32, shape, 0)
    lane = lax.broadcasted_iota(jnp.int32, shape, 1)
    rows = list(rows)
    width = GROUPS * ROWS
    for k in range(0, len(rows), GROUPS):
        first = k * ROWS
        inside = jnp.logical_and(lane >= first, lane < first + width)
        panel = rows[k : k + GROUPS]
        columns = [
            jnp.where(lane < first, -p, jnp.where(inside, 0.0, p)) for p in panel
        ]
        panel = eliminate_panel(panel, first, sub, lane)
        near = range(k + GROUPS, min(k + 2 * GROUPS, len(rows)))
        for i in near:
            terms = [
                spread(rows[i][:, first + j : first + j + 1], shape)
                * spread(panel[j // ROWS][j % ROWS : j % ROWS + 1, :], shape)
                for j in range(width)
            ]
            rows[i] = jnp.where(inside, 0.0, rows[i]) - total_of(terms)
        update = outer_product(columns, panel)
        for i in range(len(rows)):
            if i < k or i >= k + 2 * GROUPS:
                rows[i] = jnp.where(inside, 0.0, rows[i]) - update[i * ROWS : (i + 1) * ROWS, :]
        rows[k : k + GROUPS] = panel
    return rows


def invert(node, x, tile, work, late):
    half = tile.shape[0]
    top, low = slice(0, half), slice(half, 2 * half)
    tile[...] = node[0]

    @pl.loop(0, 2)
    def _(step):
        rows = spd_inverse_tile([tile[i : i + ROWS, :] for i in range(0, half, ROWS)])
        for i, row in enumerate(rows):
            tile[i * ROWS : (i + 1) * ROWS, :] = row

        @pl.when(step == 0)
        def _():
            late()
            x[top, top] = tile[...]
            work[0] = dot(tile[...], node[1])
            work[1] = work[0].T
            tile[...] = node[2] - dot(work[1], node[1])

        @pl.when(step == 1)
        def _():
            corner = -dot(tile[...], work[1])
            x[low, low] = tile[...]
            x[low, top] = corner
            x[top, low] = -dot(work[0], tile[...])
            x[top, top] = x[top, top] - dot(work[0], corner)


def kernel(
    runs,
    total,
    diag,
    coup,
    rhs,
    out,
    first_x,
    x,
    tile,
    work,
    node,
    source,
    e_turned,
    w_p,
    w_q,
    keep_p,
    keep_q,
    keep_y,
    send_d,
    send_m,
    send_t,
    send_b,
    first_d,
    first_b,
    got_d,
    got_b,
    got_link,
    got_x,
    before,
    value,
    passing,
    far_k,
    far_y,
    sent,
    sent_first,
    sent_value,
    sent_pass,
    sent_far,
    come_d,
    come_b,
    come_m,
    come_x,
    come_pass,
    come_far,
):
    slabs, order = diag.shape[:2]
    inner = slabs - 1
    half = order // 2
    top, low = slice(0, half), slice(half, order)
    me = lax.axis_index("seg") * runs + lax.axis_index("run")
    depth = total.bit_length() - 1
    strides = [1 << i for i in range(depth)]
    last = me == total - 1
    inside = jnp.logical_not(last)
    pair = lax.rem(me + 1, total // 2) == 0
    single = jnp.logical_not(pair)
    tells_last = me == total - 1 - total // 4
    reach = total // 8
    gives = lax.rem(me + 1, 4 * reach) == 2 * reach
    takes = lax.rem(me + 1, 2 * reach) == reach
    even = lax.rem(me, 2) == 0
    odd = jnp.logical_not(even)
    steps = strides[:-1]
    parents = [lax.rem(me + 1, 2 * s) == 0 for s in steps]
    level = sum(jnp.where(parent, 1, 0) for parent in parents)
    span = 1 + sum(jnp.where(parent, s, 0) for s, parent in zip(steps, parents))
    next_above = lax.rem(me + span, 4 * span) == 2 * span - 1
    up = jnp.where(next_above, 1, 0)
    peer_p = jnp.where(next_above, me + span, me - span)
    peer_q = jnp.where(next_above, me - span, me + span)
    has_q = jnp.logical_and(peer_q >= 0, peer_q < total)
    slot_p = 1 + 2 * level + (1 - up)
    slot_q = 1 + 2 * level + up
    far = jnp.where(next_above, me + 3 * reach, me - 3 * reach)
    has_far = jnp.logical_and(far >= 0, far < total)
    bends = bend_strides(runs, total)
    piece = order // PIECES

    def copy(source_ref, target_ref, send_sem, recv_sem, peer):
        return pltpu.make_async_remote_copy(
            src_ref=source_ref,
            dst_ref=target_ref,
            send_sem=send_sem,
            recv_sem=recv_sem,
            device_id=(lax.rem(peer, runs), lax.div(peer, runs)),
            device_id_type=MESH,
        )

    barrier = pltpu.get_barrier_semaphore()
    met = [lax.rem(me + 1, s) == 0 for s in strides]
    greeted = [
        (jnp.logical_and(here, ok), peer)
        for s, here in zip(strides, met)
        for ok, peer in ((me >= s, me - s), (me + s < total, me + s))
    ]
    for peer in (me - 3 * reach, me + 3 * reach):
        ok = jnp.logical_and(peer >= 0, peer < total)
        greeted.append((jnp.logical_and(lax.rem(me + 1, 4 * reach) == 0, ok), peer))
    greeted.append((jnp.logical_and(takes, has_far), far))
    for s in bends:
        greeted.append((lax.rem(me + 1, 4 * s) == 3 * s, me + s - 1))
        greeted.append((lax.rem(me + 2, 4 * s) == 0, me + 1 - s))
        greeted.append((lax.rem(me + 2, 4 * s) == 0, me + 1 - 2 * s))
        greeted.append((lax.rem(me + 1, 4 * s) == 2 * s, me + 2 * s - 1))
    peers = sum(jnp.where(ok, 1, 0) for ok, _ in greeted)
    for ok, peer in greeted:

        @pl.when(ok)
        def _():
            pl.semaphore_signal(
                barrier,
                inc=1,
                device_id=(lax.rem(peer, runs), lax.div(peer, runs)),
                device_id_type=MESH,
            )

    def first_head(peer):
        return copy(first_d.at[0], got_d.at[0, 0], sent_first.at[0], come_d.at[0], peer)

    def first_tail(peer):
        return copy(
            first_d.at[pl.ds(1, 2)], got_d.at[0, pl.ds(1, 2)], sent_first.at[1], come_d.at[1], peer
        )

    def first_link(peer):
        return copy(send_m, got_link.at[1], sent_first.at[2], come_m.at[1], peer)

    def first_thin(peer):
        return copy(first_b, got_b.at[0], sent_first.at[3], come_b.at[0], peer)

    def head(role, slot, peer):
        return copy(
            send_d.at[role, 0], got_d.at[slot, 0], sent.at[role], come_d.at[2 * slot], peer
        )

    def tail(role, slot, peer):
        return copy(
            send_d.at[role, pl.ds(1, 2)],
            got_d.at[slot, pl.ds(1, 2)],
            sent.at[2 + role],
            come_d.at[2 * slot + 1],
            peer,
        )

    def thin(role, slot, peer):
        return copy(send_b.at[role], got_b.at[slot], sent.at[4 + role], come_b.at[slot], peer)

    def coupled(side, peer):
        return copy(send_m, got_link.at[side], sent.at[6], come_m.at[side], peer)

    def mirrored():
        return copy(send_t, got_link.at[0], sent.at[7], come_m.at[0], total - 1)

    def to_bend(which, part, peer):
        rows = pl.ds(part * piece, piece)
        return copy(
            send_m.at[rows],
            passing.at[which, rows],
            sent.at[6],
            come_pass.at[which * PIECES + part],
            peer,
        )

    def from_bend(which, part, peer):
        rows = pl.ds(part * piece, piece)
        return copy(
            passing.at[which, rows],
            got_link.at[1, rows],
            sent_pass.at[which * PIECES + part],
            come_m.at[1],
            peer,
        )

    def each_gift(act):
        for way, peer in enumerate((me - reach, me + reach)):
            for k, (source_ref, target_ref) in enumerate(
                (
                    (keep_p.at[inner], far_k.at[up]),
                    (keep_q.at[inner], far_k.at[1 - up]),
                    (keep_y.at[inner], far_y),
                )
            ):
                act(copy(source_ref, target_ref, sent_far.at[3 * way + k], come_far.at[k], peer))

    def each_source(act):
        @pl.when(inside)
        def _():
            act(0, me + 1)

        for i, s in enumerate(steps):
            for way, (ok, peer) in enumerate(((me >= s, me - s), (me + s < total, me + s))):

                @pl.when(jnp.logical_and(parents[i], ok))
                def _():
                    act(1 + 2 * i + way, peer)

    e_turned[...] = jnp.where(me == 0, jnp.zeros_like(coup[0]), coup[0]).T
    node[0] = diag[0, top, top]
    node[1] = diag[0, top, low]
    node[2] = diag[0, low, low]
    source[...] = rhs[0]
    for i in range(inner):
        final = i == inner - 1
        f_turned = coup.at[i + 1]
        invert(node, first_x, tile, work, lambda: None)
        w_p[...] = dot(e_turned[...], first_x[...])

        def put(block, rows, columns):
            term = dot_nt(w_p[rows, :], e_turned[columns, :])
            first_d[block] = -term if i == 0 else first_d[block] - term

        put(0, top, top)
        if final:
            pl.semaphore_wait(barrier, peers)

            @pl.when(me > 0)
            def _():
                first_head(me - 1).start()

        put(1, top, low)
        put(2, low, low)
        if final:

            @pl.when(me > 0)
            def _():
                first_tail(me - 1).start()

        w_q[...] = dot(f_turned[...], first_x[...])
        node[0] = diag[i + 1, top, top] - dot_nt(w_q[top, :], f_turned[top, :])
        node[1] = diag[i + 1, top, low] - dot_nt(w_q[top, :], f_turned[low, :])
        node[2] = diag[i + 1, low, low] - dot_nt(w_q[low, :], f_turned[low, :])

        def rest(i):
            f_turned = coup.at[i + 1]
            keep_y[i] = dot(first_x[...], source[...])
            term = dot(e_turned[...], keep_y[i])
            first_b[...] = -term if i == 0 else first_b[...] - term
            if i == inner - 1:

                @pl.when(me > 0)
                def _():
                    first_thin(me - 1).start()

            source[...] = rhs[i + 1] - dot(f_turned[...], keep_y[i])
            keep_p[i] = dot_nt(first_x[...], e_turned[...])
            keep_q[i] = dot_nt(first_x[...], f_turned[...])

        if final:

            @pl.when(odd)
            def _():
                send_m[...] = -dot_nt(w_q[...], e_turned[...])
                first_link(me - 1).start()
                rest(inner - 1)

            @pl.when(even)
            def _():
                got_link[0] = -dot_nt(w_p[...], f_turned[...])

        else:
            rest(i)
            e_turned[...] = -dot_nt(w_p[...], f_turned[...])

    def add_head(slot, peer):
        head(0, slot, peer).wait_recv()
        node[0] = node[0] + got_d[slot, 0]

    def add_tail(slot, peer):
        tail(0, slot, peer).wait_recv()
        node[1] = node[1] + got_d[slot, 1]
        node[2] = node[2] + got_d[slot, 2]

    def add_thin(slot, peer):
        thin(0, slot, peer).wait_recv()
        source[...] = source[...] + got_b[slot]

    each_source(add_head)
    invert(node, x, tile, work, lambda: each_source(add_tail))

    def serve_head(role, slot, peer, weights, turned):
        weights[top, :] = dot(turned[top, :], x[...])
        send_d[role, 0] = -dot_nt(weights[top, :], turned[top, :])
        head(role, slot, peer).start()

    def serve_tail(role, slot, peer, weights, turned):
        send_d[role, 1] = -dot_nt(weights[top, :], turned[low, :])
        weights[low, :] = dot(turned[low, :], x[...])
        send_d[role, 2] = -dot_nt(weights[low, :], turned[low, :])
        tail(role, slot, peer).start()

    @pl.when(inside)
    def _():
        coupled(1, me + 1).wait_recv()

    @pl.when(odd)
    def _():
        coupled(0, me - 1).wait_recv()
        first_link(me - 1).wait_send()

    to_p = (0, slot_p, peer_p, w_p, got_link.at[up])
    to_q = (1, slot_q, peer_q, w_q, got_link.at[1 - up])
    serve_head(*to_p)

    @pl.when(tells_last)
    def _():
        serve_head(*to_q)

    serve_tail(*to_p)

    @pl.when(tells_last)
    def _():
        serve_tail(*to_q)

    @pl.when(single)
    def _():
        send_m[...] = -dot_nt(got_link[1 - up], w_p[...])
        bent = [lax.rem(me + 1, 4 * s) == 3 * s for s in bends]
        for i, s in enumerate(bends):

            @pl.when(bent[i])
            def _():
                for part in range(PIECES):
                    to_bend(i, part, me + s - 1).start()

        straight = sum(jnp.where(b, 1, 0) for b in bent) == 0

        @pl.when(straight)
        def _():
            coupled(1 - up, peer_p).start()

        @pl.when(tells_last)
        def _():
            send_t[...] = -dot_nt(w_p[...], got_link[1 - up])
            mirrored().start()

        keep_p[inner] = dot_nt(x[...], got_link[up])
        keep_q[inner] = dot_nt(x[...], got_link[1 - up])

    @pl.when(even)
    def _():
        rest(inner - 1)

    each_source(add_thin)
    keep_y[inner] = dot(x[...], source[...])
    send_b[0] = -dot(got_link[up], keep_y[inner])
    crosses = sum(jnp.where(lax.rem(me + 1, 4 * s) == 3 * s, 1, 0) for s in bends)

    @pl.loop(0, crosses * PAUSE_THIN)
    def _(_):
        tile[...] = tile[...].T

    thin(0, slot_p, peer_p).start()

    @pl.when(has_q)
    def _():

        @pl.when(jnp.logical_not(tells_last))
        def _():
            @pl.loop(0, jnp.where(level == 1, PAUSE, 0))
            def _(_):
                tile[...] = tile[...].T

            serve_head(*to_q)
            serve_tail(*to_q)

        send_b[1] = -dot(got_link[1 - up], keep_y[inner])
        thin(1, slot_q, peer_q).start()

    for i, s in enumerate(bends):

        @pl.when(lax.rem(me + 2, 4 * s) == 0)
        def _():
            for part in range(PIECES):
                to_bend(i, part, me).wait_recv()
                from_bend(i, part, me + 1 - 2 * s).start()

    @pl.when(gives)
    def _():
        each_gift(lambda c: c.start())

    @pl.when(single)
    def _():
        value[...] = keep_y[inner]

    @pl.when(takes)
    def _():
        for k, target_ref in enumerate((far_k.at[up], far_k.at[1 - up], far_y)):
            copy(target_ref, target_ref, sent_far.at[k], come_far.at[k], peer_p).wait_recv()
        value[...] = value[...] - dot(keep_p[inner], far_y[...])
        keep_q[inner] = keep_q[inner] - dot(keep_p[inner], far_k[1 - up])
        keep_p[inner] = -dot(keep_p[inner], far_k[up])

    passes = jnp.logical_and(level == 1, me >= 2)

    def passed(side):
        return copy(got_x.at[side], got_x.at[1], sent_pass.at[len(bends) * PIECES], come_x.at[1], me - 1)

    @pl.when(single)
    def _():
        @pl.when(has_q)
        def _():
            copy(value, got_x.at[1], sent_value.at[0], come_x.at[1], peer_q).wait_recv()

            @pl.when(jnp.logical_and(passes, up == 1))
            def _():
                passed(1).start()

            value[...] = value[...] - dot(keep_q[inner], got_x[1])

        @pl.when(jnp.logical_or(jnp.logical_not(takes), has_far))
        def _():
            copy(value, got_x.at[0], sent_value.at[0], come_x.at[0], peer_p).wait_recv()

            @pl.when(jnp.logical_and(passes, up == 0))
            def _():
                passed(0).start()

            value[...] = value[...] - dot(keep_p[inner], got_x[0])

    @pl.when(pair)
    def _():
        slot = 1 + 2 * level + up
        add_head(slot, peer_p)
        invert(node, x, tile, work, lambda: add_tail(slot, peer_p))
        add_thin(slot, peer_p)
        value[...] = dot(x[...], source[...])

    def hand_down(act):
        def near(i, s):
            role = jnp.where(jnp.logical_and(level == i + 1, inside), 0, 1)
            tells = parents[i]
            if s == reach:
                tells = jnp.logical_and(tells, jnp.logical_not(gives))
            for way, (ok, peer) in enumerate(((me >= s, me - s), (me + s < total, me + s))):
                if s == 1 and way == 1:
                    ok = jnp.logical_and(ok, level == 1)

                @pl.when(jnp.logical_and(tells, ok))
                def _():
                    act(
                        copy(
                            value, got_x.at[role], sent_value.at[2 * i + way], come_x.at[role], peer
                        )
                    )

        order_of = list(enumerate(steps))
        near(*order_of[-2])
        for way, peer in enumerate((me - 3 * reach, me + 3 * reach)):
            ok = jnp.logical_and(peer >= 0, peer < total)

            @pl.when(jnp.logical_and(lax.rem(me + 1, 4 * reach) == 0, ok))
            def _():
                act(copy(value, got_x.at[0], sent_far.at[6 + way], come_x.at[0], peer))

        near(*order_of[-1])
        for i, s in reversed(order_of[:-2]):
            near(i, s)

        @pl.when(even)
        def _():
            act(copy(value, before, sent_value.at[2 * depth], come_x.at[2], me + 1))

    hand_down(lambda c: c.start())
    out[inner] = value[...]
    for i in reversed(range(inner)):
        out[i] = keep_y[i] - dot(keep_q[i], out[i + 1])

    @pl.when(jnp.logical_and(even, me > 0))
    def _():
        for i in reversed(range(inner)):
            out[i] = out[i] - dot(keep_p[i], got_x[up])

    @pl.when(odd)
    def _():
        copy(value, before, sent_value.at[2 * depth], come_x.at[2], me - 1).wait_recv()
        for i in reversed(range(inner)):
            out[i] = out[i] - dot(keep_p[i], before[...])

    head(0, slot_p, peer_p).wait_send()
    tail(0, slot_p, peer_p).wait_send()
    thin(0, slot_p, peer_p).wait_send()

    @pl.when(single)
    def _():
        coupled(1 - up, peer_p).wait_send()

    @pl.when(tells_last)
    def _():
        mirrored().wait_send()

    @pl.when(gives)
    def _():
        each_gift(lambda c: c.wait_send())

    @pl.when(passes)
    def _():
        passed(0).wait_send()

    @pl.when(has_q)
    def _():
        head(1, slot_q, peer_q).wait_send()
        tail(1, slot_q, peer_q).wait_send()
        thin(1, slot_q, peer_q).wait_send()

    hand_down(lambda c: c.wait_send())
    for i, s in enumerate(bends):

        @pl.when(lax.rem(me + 2, 4 * s) == 0)
        def _():
            for part in range(PIECES):
                from_bend(i, part, me + 1 - 2 * s).wait_send()

    @pl.when(me > 0)
    def _():
        first_head(me - 1).wait_send()
        first_tail(me - 1).wait_send()
        first_thin(me - 1).wait_send()


def bend_strides(runs, total):
    stride = runs // 2
    return [stride] if stride > 1 and 4 * stride <= total else []


def local(runs, total, diag_blocks, coupling, rhs):
    slabs, order = diag_blocks.shape[1:3]
    half = order // 2
    columns = rhs.shape[3]
    depth = total.bit_length() - 1
    square, thin = (order, order), (order, columns)
    vmem = lambda *shape: pltpu.VMEM(shape, jnp.float32)
    dma = lambda n: pltpu.SemaphoreType.DMA((n,))
    slots = 1 + 2 * depth
    bends = len(bend_strides(runs, total))
    result = pl.pallas_call(
        functools.partial(kernel, runs, total),
        out_shape=jax.ShapeDtypeStruct(rhs.shape[1:], jnp.float32),
        in_specs=[pl.BlockSpec(memory_space=pltpu.VMEM)] * 3,
        out_specs=pl.BlockSpec(memory_space=pltpu.VMEM),
        scratch_shapes=[
            vmem(*square),
            vmem(*square),
            vmem(half, half),
            vmem(2, half, half),
            vmem(3, half, half),
            vmem(*thin),
            vmem(*square),
            vmem(*square),
            vmem(*square),
            vmem(slabs, *square),
            vmem(slabs, *square),
            vmem(slabs, *thin),
            vmem(2, 3, half, half),
            vmem(*square),
            vmem(*square),
            vmem(2, *thin),
            vmem(3, half, half),
            vmem(*thin),
            vmem(slots, 3, half, half),
            vmem(slots, *thin),
            vmem(2, *square),
            vmem(2, *thin),
            vmem(*thin),
            vmem(*thin),
            vmem(bends, *square),
            vmem(2, *square),
            vmem(*thin),
            dma(8),
            dma(4),
            dma(slots),
            dma(bends * PIECES + 1),
            dma(8),
            dma(2 * slots),
            dma(slots),
            dma(2),
            dma(3),
            dma(bends * PIECES),
            dma(3),
        ],
        compiler_params=pltpu.CompilerParams(collective_id=0, has_side_effects=True),
        name="chain_solve",
    )(diag_blocks[0], coupling[0], rhs[0])
    return result[None]


def solution(mesh):
    spec = P("seg", "run", None, None)
    runs = mesh.shape["run"]
    total = runs * mesh.shape["seg"]
    return jax.shard_map(
        functools.partial(local, runs, total),
        mesh=mesh,
        in_specs=(spec, spec, spec),
        out_specs=spec,
        check_vma=False,
    )
```
